32 devices in a mesh: rows: 2 (over x), cols: 4 (over y, core), dp: 4 (over z).
Axes of the slice: x: 2, y: 2, z: 4, core: 2. Of those that a mesh axis runs over, the one named last changes fastest.
Arguments:
- fields: float32 [128, 64, 384], P(('dp', 'rows'), 'cols'), parts along dimension 0, may hold values from -6 to 6
- logit_scale: float32 [6], replicated, may hold values from 4 to 25
- w_qkv: bfloat16 [384, 1152], replicated, may hold values from -0.3125 to 0.3125
- w_proj: bfloat16 [384, 384], replicated, may hold values from -0.3125 to 0.3125
- w_merge: bfloat16 [1536, 768], P(None, 'cols'), may hold values from -0.15625 to 0.15625
- w_up: bfloat16 [768, 3072], P('rows', 'cols'), may hold values from -0.21875 to 0.21875
- w_down: bfloat16 [3072, 768], P('cols', 'rows'), may hold values from -0.109375 to 0.109375
- cotangent: bfloat16 [64, 32, 768], P(('dp', 'rows'), 'cols'), parts along dimension 0, may hold values from -0.59765625 to 0.59765625
Outputs:
- coarse: float32 [64, 32, 768], P(('dp', 'rows'), 'cols'), parts along dimension 0
- grad_coarse: float32 [64, 32, 768], P(('dp', 'rows'), 'cols'), parts along dimension 0
- grad_up: float32 [768, 12288], P('rows', ('dp', 'cols')), parts along dimension 1
- grad_down: float32 [3072, 3072], P('cols', ('dp', 'rows')), parts along dimension 1
The draws below stay inside these ranges and needn't reach their ends.
There are 4 independent parts, one for each index of `dp`. The reference program is written for one: setup_inputs(seed, part) draws one part's arguments, and reference() takes and returns one part's arrays. A program takes and returns all parts, laid end to end along the dimension named above; an argument that names none is the same for every part. Nothing has to cross between parts.
All inputs are finite; a program needn't handle non-finite values.
Results may differ from the reference program's by a relative error of at most 0.02.
Values may be sent and summed in bfloat16 or wider, within the bound.
A program may use at most 64 MiB of HBM per device.

```python
import math
import jax
import jax.numpy as jnp
from jax import lax

C3 = 384
C4 = 768
FF4 = 3072
HEADS3 = 6
WIN = 16
NR = 32
NC = 64
N_ROWS = 2


def spiked(array, key, source, target, blocks, factor):
    def block_of(axis_at):
        return (jnp.arange(array.shape[axis_at]) // (array.shape[axis_at] // blocks)).reshape((-1,) + (1,) * (array.ndim - 1 - axis_at))

    near = jax.random.permutation(key, blocks)[block_of(target)]
    far = (block_of(target) + blocks // 2) % blocks
    return jnp.where((block_of(source) == near) | (block_of(source) == far), factor * array, array)


def block_scale(own_key, extent, cuts, least, high):
    level, own = 1.0, jax.random.fold_in(own_key, 6)
    for dim, parts in cuts:
        steps = jnp.exp(jax.random.uniform(jax.random.fold_in(own, dim), (parts,), jnp.float32, least / len(cuts), high / len(cuts)))
        level = level * jnp.repeat(steps, extent[dim] // parts).reshape([-1 if axis == dim else 1 for axis in range(len(extent))])
    return level


def gaussian(own_key, dims, deviation, most, cuts=(), kind=jnp.bfloat16):
    array = jax.random.normal(own_key, dims, jnp.float32) * deviation
    if len(cuts) > 0:
        array = block_scale(own_key, dims, cuts, -0.22, 0.18) * array
    return jnp.clip(array, min=-most, max=most).astype(kind)


def noise_with(key, extent, scale, bound, shards, heavy, dtype=jnp.bfloat16):
    entries = scale * jax.random.normal(key, extent, jnp.float32)
    if shards:
        entries = entries * block_scale(key, extent, shards, -0.22, 0.18)
    return jnp.clip(spiked(entries, jax.random.fold_in(key, 3), *heavy), -bound, bound).astype(dtype)


def setup_inputs(seed: int = 0, part: int = 0) -> dict:
    keys = jax.random.split(jax.random.key(seed), 9)
    part_keys = jax.random.split(jax.random.fold_in(keys[8], part), 9)
    return {
        "fields": gaussian(part_keys[0], (NR, NC, C3), 1.0, 6.0, ((0, 2), (1, 4)), jnp.float32),
        "logit_scale": jnp.clip(jnp.exp(jax.random.uniform(keys[1], (HEADS3,), jnp.float32, math.log(4.0), math.log(25.0))), 4.0, 25.0),
        "w_qkv": gaussian(keys[2], (C3, 3 * C3), C3 ** -0.5, 0.3125),
        "w_proj": gaussian(keys[3], (C3, C3), C3 ** -0.5, 0.3125),
        "w_merge": gaussian(keys[4], (4 * C3, C4), (4 * C3) ** -0.5, 0.15625, ((1, 4),)),
        "w_up": gaussian(keys[5], (C4, FF4), C4 ** -0.5, 0.21875, ((0, 2), (1, 4))),
        "w_down": gaussian(keys[6], (FF4, C4), FF4 ** -0.5, 0.109375, ((0, 4), (1, 2))),
        "cotangent": noise_with(part_keys[7], (NR // 2, NC // 2, C4), 0.1, 0.59765625, ((0, 2), (1, 4)), (0, 2, 2, 2.0)),
    }


eps_norm = 1e-05
eps_unit = 1e-06

def layer_norm(value):
    average = lax.optimization_barrier(jnp.mean(value, axis=-1, keepdims=True))
    centred = value - average
    spread = lax.optimization_barrier(jnp.mean(centred * centred, axis=-1, keepdims=True))
    inverse = lax.rsqrt(spread + eps_norm)
    return (centred * inverse, inverse)

def norm_slope(upstream, normed, inverse):
    first_mean = lax.optimization_barrier(jnp.mean(upstream, axis=-1, keepdims=True))
    second_mean = lax.optimization_barrier(jnp.mean(upstream * normed, axis=-1, keepdims=True))
    return inverse * (upstream - first_mean - normed * second_mean)

def unit_heads(value, head_count):
    shaped = value.reshape(value.shape[:-1] + (head_count, value.shape[-1] // head_count))
    squares = lax.optimization_barrier(jnp.sum(shaped * shaped, axis=-1, keepdims=True))
    return (shaped * lax.rsqrt(squares + eps_unit)).reshape(value.shape)

def windows_of(field_grid, window):
    grid_rows, grid_cols, channels = field_grid.shape
    shaped = field_grid.reshape(grid_rows // window, window, grid_cols // window, window, channels)
    return shaped.transpose(0, 2, 1, 3, 4).reshape(-1, window * window, channels)

def grid_of(blocks, grid_rows, grid_cols, window):
    channels = blocks.shape[-1]
    shaped = blocks.reshape(grid_rows // window, grid_cols // window, window, window, channels)
    return shaped.transpose(0, 2, 1, 3, 4).reshape(grid_rows, grid_cols, channels)

def attend_exact(queries, key_rows, value_rows, logit_scale, head_count):
    number, window_size, channels = queries.shape
    width_head = channels // head_count
    query_heads = queries.astype(jnp.float32).reshape(number, window_size, head_count, width_head)
    key_heads = key_rows.astype(jnp.float32).reshape(number, window_size, head_count, width_head)
    value_heads = value_rows.astype(jnp.float32).reshape(number, window_size, head_count, width_head)
    scores = jnp.einsum('wqhd,wkhd->whqk', query_heads, key_heads) * logit_scale[None, :, None, None]
    weights = jnp.exp(scores)
    weights = (weights / lax.optimization_barrier(jnp.sum(weights, axis=-1, keepdims=True))).astype(jnp.bfloat16)
    mixed_out = jnp.einsum('whqk,wkhd->wqhd', weights.astype(jnp.float32), value_heads)
    return mixed_out.reshape(number, window_size, channels)

def merge_patches(field_grid):
    quarters = (field_grid[0::2, 0::2], field_grid[1::2, 0::2], field_grid[0::2, 1::2], field_grid[1::2, 1::2])
    return jnp.concatenate(quarters, axis=-1)

def exact_gelu(value):
    return jax.nn.gelu(value, approximate=False)

def reference(fields, logit_scale, w_qkv, w_proj, w_merge, w_up, w_down, cotangent):
    offset = WIN // 2
    grid_rows, grid_cols, channels = fields.shape
    head_count = logit_scale.shape[0]
    rolled = jnp.roll(fields, (-offset, -offset), (0, 1)).astype(jnp.bfloat16).reshape(-1, channels)
    projected = jnp.dot(rolled, w_qkv, preferred_element_type=jnp.float32)
    queries = unit_heads(projected[:, :channels], head_count).astype(jnp.bfloat16)
    key_rows = unit_heads(projected[:, channels:2 * channels], head_count).astype(jnp.bfloat16)
    value_rows = projected[:, 2 * channels:].astype(jnp.bfloat16)

    def blocked(flat_rows):
        return windows_of(flat_rows.reshape(grid_rows, grid_cols, channels), WIN)

    def one_window(triple):
        return attend_exact(triple[0][None], triple[1][None], triple[2][None], logit_scale, head_count)[0]
    mixed = lax.map(one_window, (blocked(queries), blocked(key_rows), blocked(value_rows)))
    mixed = grid_of(mixed, grid_rows, grid_cols, WIN)
    mixed = jnp.roll(mixed, (offset, offset), (0, 1)).astype(jnp.bfloat16).reshape(-1, channels)
    branch = jnp.dot(mixed, w_proj, preferred_element_type=jnp.float32)
    normed, _ = layer_norm(branch)
    stream = fields + normed.reshape(fields.shape)
    merged = merge_patches(stream).astype(jnp.bfloat16)
    coarse_rows, coarse_cols = (merged.shape[0], merged.shape[1])
    merged_rows = merged.reshape(-1, merged.shape[-1])
    level, _ = layer_norm(jnp.dot(merged_rows, w_merge, preferred_element_type=jnp.float32))
    level_b = level.astype(jnp.bfloat16)
    hidden_pre = jnp.dot(level_b, w_up, preferred_element_type=jnp.float32)
    hidden = exact_gelu(hidden_pre).astype(jnp.bfloat16)
    branch_out = jnp.dot(hidden, w_down, preferred_element_type=jnp.float32)
    branch_norm, branch_inv = layer_norm(branch_out)
    coarse = level + branch_norm
    upstream = cotangent.astype(jnp.float32).reshape(coarse.shape)
    slope_out = norm_slope(upstream, branch_norm, branch_inv).astype(jnp.bfloat16)
    slope_hidden = jnp.dot(slope_out, w_down.T, preferred_element_type=jnp.float32)
    _, pullback = jax.vjp(exact_gelu, hidden_pre)
    slope_pre = pullback(slope_hidden)[0].astype(jnp.bfloat16)
    grad_coarse = upstream + jnp.dot(slope_pre, w_up.T, preferred_element_type=jnp.float32)

    def banded(value):
        return value.reshape(N_ROWS, -1, value.shape[-1])

    def add_band(running, items):
        inputs_band, pre_band, hidden_band, out_band = items
        term_up = jnp.dot(inputs_band.T, pre_band, preferred_element_type=jnp.float32)
        term_down = jnp.dot(hidden_band.T, out_band, preferred_element_type=jnp.float32)
        term_up = lax.optimization_barrier(term_up.astype(jnp.bfloat16)).astype(jnp.float32)
        term_down = lax.optimization_barrier(term_down.astype(jnp.bfloat16)).astype(jnp.float32)
        return ((running[0] + term_up, running[1] + term_down), None)
    start_up = jnp.zeros((w_up.shape[0], w_up.shape[1]), jnp.float32)
    start_down = jnp.zeros((w_down.shape[0], w_down.shape[1]), jnp.float32)
    (grad_up, grad_down), _ = lax.scan(add_band, (start_up, start_down), (banded(level_b), banded(slope_pre), banded(hidden), banded(slope_out)))
    return (coarse.reshape(coarse_rows, coarse_cols, -1), grad_coarse.reshape(coarse_rows, coarse_cols, -1), grad_up, grad_down)
```

```python
import jax
import jax.numpy as jnp
import numpy as np
from jax import lax
from jax.experimental import pallas as pl
from jax.experimental.pallas import tpu as pltpu
from jax.sharding import PartitionSpec as P

WIN = 16


eps_norm = 1e-05
eps_unit = 1e-06


def padded_2(cells, sides, width):
    for axis, dim in sides:
        count = lax.axis_size(axis)
        head = lax.slice_in_dim(cells, 0, width, axis=dim)
        tail = lax.slice_in_dim(cells, cells.shape[dim] - width, cells.shape[dim], axis=dim)
        cells = jnp.concatenate(
            [
                lax.ppermute(tail, axis, [(i, (i + 1) % count) for i in range(count)]),
                cells,
                lax.ppermute(head, axis, [((i + 1) % count, i) for i in range(count)]),
            ],
            axis=dim,
        )
    return cells


def layer_norm(value):
    average = jnp.mean(value, axis=-1, keepdims=True)
    centred = value - average
    spread = jnp.mean(centred * centred, axis=-1, keepdims=True)
    inverse = lax.rsqrt(spread + eps_norm)
    return (centred * inverse, inverse)


def norm_slope(upstream, normed, inverse):
    first_mean = jnp.mean(upstream, axis=-1, keepdims=True)
    second_mean = jnp.mean(upstream * normed, axis=-1, keepdims=True)
    return inverse * (upstream - first_mean - normed * second_mean)


def unit_heads(value, head_count):
    shaped = value.reshape(value.shape[:-1] + (head_count, value.shape[-1] // head_count))
    squares = jnp.sum(shaped * shaped, axis=-1, keepdims=True)
    return (shaped * lax.rsqrt(squares + eps_unit)).reshape(value.shape)


def windows_of(field_grid, window):
    grid_rows, grid_cols, channels = field_grid.shape
    shaped = field_grid.reshape(grid_rows // window, window, grid_cols // window, window, channels)
    return shaped.transpose(0, 2, 1, 3, 4).reshape(-1, window * window, channels)


def grid_of(blocks, grid_rows, grid_cols, window):
    channels = blocks.shape[-1]
    shaped = blocks.reshape(grid_rows // window, grid_cols // window, window, window, channels)
    return shaped.transpose(0, 2, 1, 3, 4).reshape(grid_rows, grid_cols, channels)


def attend(queries, key_rows, value_rows, logit_scale, head_count):
    number, window_size, channels = queries.shape
    width_head = channels // head_count
    query_heads = queries.reshape(number, window_size, head_count, width_head)
    key_heads = key_rows.reshape(number, window_size, head_count, width_head)
    value_heads = value_rows.reshape(number, window_size, head_count, width_head)
    scores = jnp.einsum(
        "wqhd,wkhd->whqk", query_heads, key_heads, preferred_element_type=jnp.float32
    )
    weights = jnp.exp(scores * logit_scale[None, :, None, None])
    weights = (weights / jnp.sum(weights, axis=-1, keepdims=True)).astype(jnp.bfloat16)
    mixed_out = jnp.einsum(
        "whqk,wkhd->wqhd", weights, value_heads, preferred_element_type=jnp.float32
    )
    return mixed_out.reshape(number, window_size, channels)


def merge_patches(field_grid):
    quarters = (
        field_grid[0::2, 0::2],
        field_grid[1::2, 0::2],
        field_grid[0::2, 1::2],
        field_grid[1::2, 1::2],
    )
    return jnp.concatenate(quarters, axis=-1)


def exact_gelu(value):
    return jax.nn.gelu(value, approximate=False)


def local(fields, logit_scale, w_qkv, w_proj, w_merge, w_up, w_down, cotangent):
    tile_rows, tile_cols, channels = fields.shape
    offset = WIN // 2
    head_count = logit_scale.shape[0]
    tokens = fields.astype(jnp.bfloat16)
    token_rows = tokens.reshape(-1, channels)
    wide_rows = tile_rows + WIN
    wide_cols = tile_cols + WIN
    widened = padded_2(tokens, (("rows", 0), ("cols", 1)), offset)
    wide_proj = jnp.dot(
        widened.reshape(-1, channels), w_qkv[:, channels:], preferred_element_type=jnp.float32
    )
    key_grid = unit_heads(wide_proj[:, :channels], head_count).astype(jnp.bfloat16)
    value_grid = wide_proj[:, channels:].astype(jnp.bfloat16)
    query_raw = jnp.dot(token_rows, w_qkv[:, :channels], preferred_element_type=jnp.float32)
    queries = (
        unit_heads(query_raw, head_count)
        .astype(jnp.bfloat16)
        .reshape(tile_rows, tile_cols, channels)
    )
    padded = jnp.pad(queries, ((offset, offset), (offset, offset), (0, 0)))
    key_blocks = windows_of(key_grid.reshape(wide_rows, wide_cols, channels), WIN)
    value_blocks = windows_of(value_grid.reshape(wide_rows, wide_cols, channels), WIN)
    mixed = attend(windows_of(padded, WIN), key_blocks, value_blocks, logit_scale, head_count)
    mixed = grid_of(mixed, wide_rows, wide_cols, WIN)[
        offset : offset + tile_rows, offset : offset + tile_cols
    ]
    mixed = mixed.astype(jnp.bfloat16).reshape(-1, channels)
    normed, _ = layer_norm(jnp.dot(mixed, w_proj, preferred_element_type=jnp.float32))
    stream = fields + normed.reshape(fields.shape)
    merged = merge_patches(stream).astype(jnp.bfloat16)
    merged_rows = merged.reshape(-1, merged.shape[-1])
    own_count = merged_rows.shape[0]
    partial_band = jnp.dot(
        lax.all_gather(merged_rows, "cols", axis=0, tiled=True),
        w_merge,
        preferred_element_type=jnp.float32,
    )
    projected_band = lax.all_gather(
        partial_band.astype(jnp.bfloat16), "cols", axis=1, tiled=True
    ).astype(partial_band.dtype)
    level_band, _ = layer_norm(projected_band)
    level_b = level_band.astype(jnp.bfloat16)
    level_own = lax.dynamic_slice_in_dim(
        level_band, lax.axis_index("cols") * own_count, own_count, 0
    )
    up_full = lax.all_gather(w_up, "rows", axis=0, tiled=True)
    down_full = lax.all_gather(w_down, "rows", axis=1, tiled=True)
    hidden_pre = jnp.dot(level_b, up_full, preferred_element_type=jnp.float32)
    hidden = exact_gelu(hidden_pre).astype(jnp.bfloat16)
    rows_part = hidden
    branch_out = lax.psum_scatter(
        jnp.dot(rows_part, down_full, preferred_element_type=jnp.float32).astype(jnp.bfloat16),
        "cols",
        scatter_dimension=0,
        tiled=True,
    ).astype(jnp.float32)
    branch_norm, branch_inv = layer_norm(branch_out)
    coarse = level_own + branch_norm
    upstream = cotangent.astype(jnp.float32).reshape(own_count, -1)
    slope_own = norm_slope(upstream, branch_norm, branch_inv).astype(jnp.bfloat16)
    slope_out = lax.all_gather(slope_own, "cols", axis=0, tiled=True)
    slope_hidden = jnp.einsum("tc,fc->tf", slope_out, down_full, preferred_element_type=jnp.float32)
    _, pullback = jax.vjp(exact_gelu, hidden_pre)
    slope_pre = pullback(slope_hidden)[0].astype(jnp.bfloat16)
    rows_part = slope_pre
    slope_input = lax.psum_scatter(
        jnp.einsum("tf,cf->tc", rows_part, up_full, preferred_element_type=jnp.float32).astype(
            jnp.bfloat16
        ),
        "cols",
        scatter_dimension=0,
        tiled=True,
    ).astype(jnp.float32)
    grad_coarse = upstream + slope_input
    term_up = jnp.einsum("tc,tf->cf", level_b, slope_pre, preferred_element_type=jnp.float32)
    term_down = jnp.einsum("tf,tc->fc", hidden, slope_out, preferred_element_type=jnp.float32)
    grad_up, grad_down = (
        lax.psum_scatter(
            term_up.astype(jnp.bfloat16), "rows", scatter_dimension=0, tiled=True
        ).astype(jnp.float32),
        lax.psum_scatter(
            term_down.astype(jnp.bfloat16), "rows", scatter_dimension=1, tiled=True
        ).astype(jnp.float32),
    )
    coarse_shape = (tile_rows // 2, tile_cols // 2, coarse.shape[-1])
    return (coarse.reshape(coarse_shape), grad_coarse.reshape(coarse_shape), grad_up, grad_down)


def _ln(value):
    average = jnp.mean(value, axis=-1, keepdims=True)
    centred = value - average
    spread = jnp.mean(centred * centred, axis=-1, keepdims=True)
    inverse = lax.rsqrt(spread + eps_norm)
    return centred * inverse, inverse


def _dot(a, b, ca=1, cb=0):
    return lax.dot_general(
        a, b, (((ca,), (cb,)), ((), ())), preferred_element_type=jnp.float32
    )


def fused_kernel(
    fields, logit, w_qkv, w_proj, w_merge, w_up, w_down, cot,
    coarse, gcoarse, gup, gdown,
    sendq, winq, mixw, mixq, wm, up, down, lvl, hid, dgel, bsend, brecv, slo, spre, gsend, grecv,
    lvl_p, hid_p, slo_p, spre_p,
    loc, s_q, r_q, s_b, r_b, s_w, r_w, s_l, r_l, s_d, r_d, s_s, r_s, s_g, r_g, s_p, r_p,
):
    f32, bf16 = jnp.float32, jnp.bfloat16
    i, j = lax.axis_index("rows"), lax.axis_index("cols")
    ni, nj = lax.axis_size("rows"), lax.axis_size("cols")
    half_side = WIN // 2
    quad = half_side * half_side
    ch = fields.shape[-1]
    c4 = cot.shape[-1]
    own = cot.shape[0]
    half = c4 // ni
    heads = logit.shape[0]
    width = ch // heads
    other = (i + 1) % ni
    prev_j, next_j = (j + nj - 1) % nj, (j + 1) % nj
    partner = j + 1 - 2 * (j % 2)
    far = (j + 2) % nj
    far_partner = (partner + 2) % nj
    peers = (partner, far, far_partner)

    def remote(src, dst, send, recv, row, col):
        return pltpu.make_async_remote_copy(
            src_ref=src, dst_ref=dst, send_sem=send, recv_sem=recv,
            device_id={"rows": row, "cols": col}, device_id_type=pl.DeviceIdType.MESH,
        )

    def quarter(a, b):
        part = fields[a * half_side:(a + 1) * half_side, b * half_side:(b + 1) * half_side, :]
        return part.reshape(quad, ch)

    for k in range(3):
        sendq[k] = quarter(k // 2, k % 2).astype(bf16)
    winq[3] = quarter(1, 1).astype(bf16)

    barrier = pltpu.get_barrier_semaphore()
    greet = [(i, p) for p in peers] + [(other, j), (other, prev_j), (other, next_j)]
    for row, col in greet:
        pl.semaphore_signal(
            barrier, inc=1, device_id={"rows": row, "cols": col},
            device_id_type=pl.DeviceIdType.MESH,
        )
    pl.semaphore_wait(barrier, len(greet))

    targets = ((other, prev_j), (other, j), (i, prev_j))
    backs = ((other, next_j), (other, j), (i, next_j))
    quads = [
        remote(sendq.at[k], winq.at[k], s_q.at[k], r_q.at[k], *targets[k]) for k in range(3)
    ]
    for c in quads:
        c.start()
    up_rows = pl.ds(pl.multiple_of(i * half, 128), half)
    merge_out = [
        remote(w_merge, wm.at[j], s_w.at[0], r_w.at[0], i, far),
        remote(w_merge, wm.at[j], s_w.at[1], r_w.at[1], i, partner),
    ]
    weights_out = [
        remote(w_up, up.at[up_rows, :], s_w.at[2], r_w.at[2], other, j),
        remote(w_down, down.at[i], s_w.at[3], r_w.at[3], other, j),
    ]
    for c in merge_out + weights_out:
        c.start()
    locals_ = [
        pltpu.make_async_copy(w_merge, wm.at[j], loc.at[0]),
        pltpu.make_async_copy(w_up, up.at[up_rows, :], loc.at[1]),
        pltpu.make_async_copy(w_down, down.at[i], loc.at[2]),
    ]
    for c in locals_:
        c.start()

    lane = lax.broadcasted_iota(jnp.int32, (ch, ch), 0) // width
    lane_t = lax.broadcasted_iota(jnp.int32, (ch, ch), 1) // width
    block_ones = (lane == lane_t).astype(f32).astype(bf16)

    def unit(value):
        squares = value * value
        top = squares.astype(bf16)
        low = (squares - top.astype(f32)).astype(bf16)
        total = _dot(top, block_ones) + _dot(low, block_ones)
        return (value * lax.rsqrt(total + eps_unit)).astype(bf16)

    for c in quads:
        c.wait_recv()
    tokens = winq[...].reshape(4 * quad, ch)
    qhat = unit(_dot(tokens, w_qkv[:, :ch]))
    khat = unit(_dot(tokens, w_qkv[:, ch:2 * ch]))
    vals = _dot(tokens, w_qkv[:, 2 * ch:]).astype(bf16)
    per = 128 // width
    lanes = lax.broadcasted_iota(jnp.int32, (4 * quad, 128), 1) // width
    for b in range(ch // 128):
        cut = slice(b * 128, (b + 1) * 128)
        qb, kb, vb = qhat[:, cut], khat[:, cut], vals[:, cut]
        acc = None
        for t in range(per):
            mine = lanes == t
            zero = jnp.zeros_like(qb)
            scores = _dot(jnp.where(mine, qb, zero), kb, 1, 1) * logit[b * per + t]
            weights = jnp.exp(scores)
            weights = (weights / jnp.sum(weights, axis=-1, keepdims=True)).astype(bf16)
            term = _dot(weights, jnp.where(mine, vb, zero))
            acc = term if acc is None else acc + term
        mixw[:, :, cut] = acc.astype(bf16).reshape(4, quad, 128)
    returns = [
        remote(mixw.at[k], mixq.at[k], s_b.at[k], r_b.at[k], *backs[k]) for k in range(3)
    ]
    for c in returns:
        c.start()
    mixq[3] = mixw[3]
    merge_out[0].wait_recv()
    onward = remote(wm.at[far], wm.at[far], s_w.at[4], r_w.at[4], i, partner)
    onward.start()
    rows_out = lax.broadcasted_iota(jnp.int32, (4 * quad, 4 * quad), 0)
    cols_in = lax.broadcasted_iota(jnp.int32, (4 * quad, 4 * quad), 1)
    which, place = rows_out // quad, rows_out % quad
    r = 2 * (place // half_side) + which % 2
    c = 2 * (place % half_side) + which // 2
    source = ((r // half_side) * 2 + c // half_side) * quad + (r % half_side) * half_side + c % half_side
    permute = (source == cols_in).astype(f32).astype(bf16)
    for cp in returns:
        cp.wait_recv()
    normed, _ = _ln(_dot(mixq[...].reshape(4 * quad, ch), w_proj[...]))
    flat = jnp.concatenate([quarter(k // 2, k % 2) for k in range(4)], axis=0)
    stream = (flat + normed).astype(bf16)
    picked = _dot(permute, stream).astype(bf16)
    merged = jnp.concatenate([picked[k * quad:(k + 1) * quad] for k in range(4)], axis=1)
    locals_[0].wait()
    merge_out[1].wait_recv()
    onward.wait_recv()
    projected = jnp.concatenate([_dot(merged, wm[k]) for k in range(nj)], axis=1)
    level, _ = _ln(projected)
    lvl[j] = level.astype(bf16)
    level_out = [
        remote(lvl.at[j], lvl.at[j], s_l.at[k], r_l.at[k], i, peers[k]) for k in range(3)
    ]
    for cp in level_out:
        cp.start()
    locals_[1].wait()
    locals_[2].wait()
    weights_out[0].wait_recv()

    pair = j // 2
    pairs = (pair, (pair + 1) % 2)

    def rows_of(p):
        return pl.ds(pl.multiple_of(p * 2 * own, 128), 2 * own)

    branch_out = []
    own_rows = None
    for t in range(2):
        p = pairs[t]
        if t == 0:
            level_out[0].wait_recv()
        else:
            level_out[1].wait_recv()
            level_out[2].wait_recv()
        pre = _dot(lvl[pl.ds(p * 2, 2)].reshape(2 * own, c4), up[...])
        cdf = 0.5 * (1.0 + lax.erf(pre * np.float32(np.sqrt(0.5))))
        hidden = (pre * cdf).astype(bf16)
        hid[rows_of(p), :] = hidden
        dgel[rows_of(p), :] = cdf + pre * (jnp.exp(-0.5 * pre * pre) * np.float32(1 / np.sqrt(2 * np.pi)))
        if t == 0:
            weights_out[1].wait_recv()
        out = jnp.concatenate([_dot(hidden, down[k]) for k in range(ni)], axis=1)
        bsend[pl.ds(p * 2, 2)] = out.astype(bf16).reshape(2, own, c4)
        for k in ((0,) if t == 0 else (1, 2)):
            cp = remote(bsend.at[peers[k]], brecv.at[j], s_d.at[k], r_d.at[k], i, peers[k])
            cp.start()
            branch_out.append(cp)
    back_half = pl.ds(pl.multiple_of(other * half, 128), half)
    my_half = pl.ds(pl.multiple_of(i * half, 128), half)
    across = [
        remote(lvl.at[:, :, back_half], lvl_p, s_p.at[0], r_p.at[0], other, j),
        remote(hid, hid_p, s_p.at[1], r_p.at[1], other, j),
    ]
    for cp in across:
        cp.start()
    total = bsend[j].astype(f32)
    for k in range(3):
        branch_out[k].wait_recv()
        total = total + brecv[peers[k]].astype(f32)
    norm, inverse = _ln(total)
    coarse[...] = level + norm
    g = cot[...].astype(f32)
    slope = inverse * (
        g - jnp.mean(g, axis=-1, keepdims=True) - norm * jnp.mean(g * norm, axis=-1, keepdims=True)
    )
    slo[j] = slope.astype(bf16)
    slope_out = [
        remote(slo.at[j], slo.at[j], s_s.at[k], r_s.at[k], i, peers[k]) for k in range(3)
    ]
    for cp in slope_out:
        cp.start()
    grad_out = []
    for t in range(2):
        p = pairs[t]
        if t == 0:
            slope_out[0].wait_recv()
        else:
            slope_out[1].wait_recv()
            slope_out[2].wait_recv()
        so = slo[pl.ds(p * 2, 2)].reshape(2 * own, c4)
        back = _dot(so[:, :half], down[0], 1, 1)
        for k in range(1, ni):
            back = back + _dot(so[:, k * half:(k + 1) * half], down[k], 1, 1)
        sp = (dgel[rows_of(p), :] * back).astype(bf16)
        spre[rows_of(p), :] = sp
        out = _dot(sp, up[...], 1, 1)
        gsend[pl.ds(p * 2, 2)] = out.astype(bf16).reshape(2, own, c4)
        for k in ((0,) if t == 0 else (1, 2)):
            cp = remote(gsend.at[peers[k]], grecv.at[j], s_g.at[k], r_g.at[k], i, peers[k])
            cp.start()
            grad_out.append(cp)
    across += [
        remote(spre, spre_p, s_p.at[3], r_p.at[3], other, j),
        remote(slo.at[:, :, back_half], slo_p, s_p.at[2], r_p.at[2], other, j),
    ]
    across[2].start()
    across[3].start()
    hid_all = hid[...]
    gdown[...] = _dot(hid_all, slo[:, :, my_half].reshape(4 * own, half), 0, 0)
    gup[...] = _dot(lvl[:, :, my_half].reshape(4 * own, half), spre[...], 0, 0)
    total = gsend[j].astype(f32)
    for k in range(3):
        grad_out[k].wait_recv()
        total = total + grecv[peers[k]].astype(f32)
    gcoarse[...] = g + total
    across[0].wait_recv()
    across[1].wait_recv()
    across[3].wait_recv()
    gdown[...] += _dot(hid_p[...], slo_p[...].reshape(4 * own, half), 0, 0)
    across[2].wait_recv()
    gup[...] += _dot(lvl_p[...].reshape(4 * own, half), spre_p[...], 0, 0)
    sent = quads + merge_out + weights_out + returns + [onward] + level_out
    for cp in sent + branch_out + slope_out + grad_out + across:
        cp.wait_send()


def fused(fields, logit_scale, w_qkv, w_proj, w_merge, w_up, w_down, cotangent):
    tile_rows, tile_cols, ch = fields.shape
    ni, nj = lax.axis_size("rows"), lax.axis_size("cols")
    own = cotangent.shape[0] * cotangent.shape[1]
    c4 = cotangent.shape[-1]
    half, ff = w_up.shape
    f32, bf16 = jnp.float32, jnp.bfloat16
    quad = (WIN // 2) ** 2
    vm = pl.BlockSpec(memory_space=pltpu.VMEM)
    hb = pl.BlockSpec(memory_space=pl.ANY)
    dma = pltpu.SemaphoreType.DMA
    band = nj * own
    outs = pl.pallas_call(
        fused_kernel,
        out_shape=(
            jax.ShapeDtypeStruct((own, c4), f32),
            jax.ShapeDtypeStruct((own, c4), f32),
            jax.ShapeDtypeStruct((half, ff), f32),
            jax.ShapeDtypeStruct((ff, half), f32),
        ),
        in_specs=[vm, pl.BlockSpec(memory_space=pltpu.SMEM), vm, vm, hb, hb, hb, vm],
        out_specs=(vm, vm, vm, vm),
        scratch_shapes=[
            pltpu.VMEM((3, quad, ch), bf16),
            pltpu.VMEM((4, quad, ch), bf16),
            pltpu.VMEM((4, quad, ch), bf16),
            pltpu.VMEM((4, quad, ch), bf16),
            pltpu.VMEM((nj,) + w_merge.shape, bf16),
            pltpu.VMEM((c4, ff), bf16),
            pltpu.VMEM((ni, ff, half), bf16),
            pltpu.VMEM((nj, own, c4), bf16),
            pltpu.VMEM((band, ff), bf16),
            pltpu.VMEM((band, ff), f32),
            pltpu.VMEM((nj, own, c4), bf16),
            pltpu.VMEM((nj, own, c4), bf16),
            pltpu.VMEM((nj, own, c4), bf16),
            pltpu.VMEM((band, ff), bf16),
            pltpu.VMEM((nj, own, c4), bf16),
            pltpu.VMEM((nj, own, c4), bf16),
            pltpu.VMEM((nj, own, half), bf16),
            pltpu.VMEM((band, ff), bf16),
            pltpu.VMEM((nj, own, half), bf16),
            pltpu.VMEM((band, ff), bf16),
            dma((3,)),
            dma((3,)), dma((3,)), dma((3,)), dma((3,)), dma((5,)), dma((5,)),
            dma((3,)), dma((3,)), dma((3,)), dma((3,)), dma((3,)), dma((3,)),
            dma((3,)), dma((3,)), dma((4,)), dma((4,)),
        ],
        compiler_params=pltpu.CompilerParams(collective_id=0, has_side_effects=True),
    )(fields, logit_scale, w_qkv, w_proj, w_merge, w_up, w_down, cotangent.reshape(own, c4))
    shape = (tile_rows // 2, tile_cols // 2, c4)
    return outs[0].reshape(shape), outs[1].reshape(shape), outs[2], outs[3]


def device_body(*args):
    fields, _, w_qkv, _, w_merge, w_up, w_down, _ = args
    fits = (
        lax.axis_size("rows") == 2
        and lax.axis_size("cols") == 4
        and fields.shape[:2] == (WIN, WIN)
        and w_up.shape[0] % 128 == 0
        and fields.shape[-1] % 128 == 0
    )
    return fused(*args) if fits else local(*args)


def solution(mesh):
    return jax.shard_map(
        device_body,
        mesh=mesh,
        in_specs=(
            P(("dp", "rows"), "cols", None),
            P(),
            P(),
            P(),
            P(None, "cols"),
            P("rows", "cols"),
            P("cols", "rows"),
            P(("dp", "rows"), "cols", None),
        ),
        out_specs=(
            P(("dp", "rows"), "cols", None),
            P(("dp", "rows"), "cols", None),
            P("rows", ("dp", "cols")),
            P("cols", ("dp", "rows")),
        ),
        check_vma=False,
    )
```

```python
import jax
import jax.numpy as jnp
import numpy as np
from jax import lax
from jax.experimental import pallas as pl
from jax.experimental.pallas import tpu as pltpu
from jax.sharding import PartitionSpec as P

WIN = 16


eps_norm = 1e-05
eps_unit = 1e-06


def padded_2(cells, sides, width):
    for axis, dim in sides:
        count = lax.axis_size(axis)
        head = lax.slice_in_dim(cells, 0, width, axis=dim)
        tail = lax.slice_in_dim(cells, cells.shape[dim] - width, cells.shape[dim], axis=dim)
        cells = jnp.concatenate(
            [
                lax.ppermute(tail, axis, [(i, (i + 1) % count) for i in range(count)]),
                cells,
                lax.ppermute(head, axis, [((i + 1) % count, i) for i in range(count)]),
            ],
            axis=dim,
        )
    return cells


def layer_norm(value):
    average = jnp.mean(value, axis=-1, keepdims=True)
    centred = value - average
    spread = jnp.mean(centred * centred, axis=-1, keepdims=True)
    inverse = lax.rsqrt(spread + eps_norm)
    return (centred * inverse, inverse)


def norm_slope(upstream, normed, inverse):
    first_mean = jnp.mean(upstream, axis=-1, keepdims=True)
    second_mean = jnp.mean(upstream * normed, axis=-1, keepdims=True)
    return inverse * (upstream - first_mean - normed * second_mean)


def unit_heads(value, head_count):
    shaped = value.reshape(value.shape[:-1] + (head_count, value.shape[-1] // head_count))
    squares = jnp.sum(shaped * shaped, axis=-1, keepdims=True)
    return (shaped * lax.rsqrt(squares + eps_unit)).reshape(value.shape)


def windows_of(field_grid, window):
    grid_rows, grid_cols, channels = field_grid.shape
    shaped = field_grid.reshape(grid_rows // window, window, grid_cols // window, window, channels)
    return shaped.transpose(0, 2, 1, 3, 4).reshape(-1, window * window, channels)


def grid_of(blocks, grid_rows, grid_cols, window):
    channels = blocks.shape[-1]
    shaped = blocks.reshape(grid_rows // window, grid_cols // window, window, window, channels)
    return shaped.transpose(0, 2, 1, 3, 4).reshape(grid_rows, grid_cols, channels)


def attend(queries, key_rows, value_rows, logit_scale, head_count):
    number, window_size, channels = queries.shape
    width_head = channels // head_count
    query_heads = queries.reshape(number, window_size, head_count, width_head)
    key_heads = key_rows.reshape(number, window_size, head_count, width_head)
    value_heads = value_rows.reshape(number, window_size, head_count, width_head)
    scores = jnp.einsum(
        "wqhd,wkhd->whqk", query_heads, key_heads, preferred_element_type=jnp.float32
    )
    weights = jnp.exp(scores * logit_scale[None, :, None, None])
    weights = (weights / jnp.sum(weights, axis=-1, keepdims=True)).astype(jnp.bfloat16)
    mixed_out = jnp.einsum(
        "whqk,wkhd->wqhd", weights, value_heads, preferred_element_type=jnp.float32
    )
    return mixed_out.reshape(number, window_size, channels)


def merge_patches(field_grid):
    quarters = (
        field_grid[0::2, 0::2],
        field_grid[1::2, 0::2],
        field_grid[0::2, 1::2],
        field_grid[1::2, 1::2],
    )
    return jnp.concatenate(quarters, axis=-1)


def exact_gelu(value):
    return jax.nn.gelu(value, approximate=False)


def local(fields, logit_scale, w_qkv, w_proj, w_merge, w_up, w_down, cotangent):
    tile_rows, tile_cols, channels = fields.shape
    offset = WIN // 2
    head_count = logit_scale.shape[0]
    tokens = fields.astype(jnp.bfloat16)
    token_rows = tokens.reshape(-1, channels)
    wide_rows = tile_rows + WIN
    wide_cols = tile_cols + WIN
    widened = padded_2(tokens, (("rows", 0), ("cols", 1)), offset)
    wide_proj = jnp.dot(
        widened.reshape(-1, channels), w_qkv[:, channels:], preferred_element_type=jnp.float32
    )
    key_grid = unit_heads(wide_proj[:, :channels], head_count).astype(jnp.bfloat16)
    value_grid = wide_proj[:, channels:].astype(jnp.bfloat16)
    query_raw = jnp.dot(token_rows, w_qkv[:, :channels], preferred_element_type=jnp.float32)
    queries = (
        unit_heads(query_raw, head_count)
        .astype(jnp.bfloat16)
        .reshape(tile_rows, tile_cols, channels)
    )
    padded = jnp.pad(queries, ((offset, offset), (offset, offset), (0, 0)))
    key_blocks = windows_of(key_grid.reshape(wide_rows, wide_cols, channels), WIN)
    value_blocks = windows_of(value_grid.reshape(wide_rows, wide_cols, channels), WIN)
    mixed = attend(windows_of(padded, WIN), key_blocks, value_blocks, logit_scale, head_count)
    mixed = grid_of(mixed, wide_rows, wide_cols, WIN)[
        offset : offset + tile_rows, offset : offset + tile_cols
    ]
    mixed = mixed.astype(jnp.bfloat16).reshape(-1, channels)
    normed, _ = layer_norm(jnp.dot(mixed, w_proj, preferred_element_type=jnp.float32))
    stream = fields + normed.reshape(fields.shape)
    merged = merge_patches(stream).astype(jnp.bfloat16)
    merged_rows = merged.reshape(-1, merged.shape[-1])
    own_count = merged_rows.shape[0]
    partial_band = jnp.dot(
        lax.all_gather(merged_rows, "cols", axis=0, tiled=True),
        w_merge,
        preferred_element_type=jnp.float32,
    )
    projected_band = lax.all_gather(
        partial_band.astype(jnp.bfloat16), "cols", axis=1, tiled=True
    ).astype(partial_band.dtype)
    level_band, _ = layer_norm(projected_band)
    level_b = level_band.astype(jnp.bfloat16)
    level_own = lax.dynamic_slice_in_dim(
        level_band, lax.axis_index("cols") * own_count, own_count, 0
    )
    up_full = lax.all_gather(w_up, "rows", axis=0, tiled=True)
    down_full = lax.all_gather(w_down, "rows", axis=1, tiled=True)
    hidden_pre = jnp.dot(level_b, up_full, preferred_element_type=jnp.float32)
    hidden = exact_gelu(hidden_pre).astype(jnp.bfloat16)
    rows_part = hidden
    branch_out = lax.psum_scatter(
        jnp.dot(rows_part, down_full, preferred_element_type=jnp.float32).astype(jnp.bfloat16),
        "cols",
        scatter_dimension=0,
        tiled=True,
    ).astype(jnp.float32)
    branch_norm, branch_inv = layer_norm(branch_out)
    coarse = level_own + branch_norm
    upstream = cotangent.astype(jnp.float32).reshape(own_count, -1)
    slope_own = norm_slope(upstream, branch_norm, branch_inv).astype(jnp.bfloat16)
    slope_out = lax.all_gather(slope_own, "cols", axis=0, tiled=True)
    slope_hidden = jnp.einsum("tc,fc->tf", slope_out, down_full, preferred_element_type=jnp.float32)
    _, pullback = jax.vjp(exact_gelu, hidden_pre)
    slope_pre = pullback(slope_hidden)[0].astype(jnp.bfloat16)
    rows_part = slope_pre
    slope_input = lax.psum_scatter(
        jnp.einsum("tf,cf->tc", rows_part, up_full, preferred_element_type=jnp.float32).astype(
            jnp.bfloat16
        ),
        "cols",
        scatter_dimension=0,
        tiled=True,
    ).astype(jnp.float32)
    grad_coarse = upstream + slope_input
    term_up = jnp.einsum("tc,tf->cf", level_b, slope_pre, preferred_element_type=jnp.float32)
    term_down = jnp.einsum("tf,tc->fc", hidden, slope_out, preferred_element_type=jnp.float32)
    grad_up, grad_down = (
        lax.psum_scatter(
            term_up.astype(jnp.bfloat16), "rows", scatter_dimension=0, tiled=True
        ).astype(jnp.float32),
        lax.psum_scatter(
            term_down.astype(jnp.bfloat16), "rows", scatter_dimension=1, tiled=True
        ).astype(jnp.float32),
    )
    coarse_shape = (tile_rows // 2, tile_cols // 2, coarse.shape[-1])
    return (coarse.reshape(coarse_shape), grad_coarse.reshape(coarse_shape), grad_up, grad_down)


def _ln(value):
    average = jnp.mean(value, axis=-1, keepdims=True)
    centred = value - average
    spread = jnp.mean(centred * centred, axis=-1, keepdims=True)
    inverse = lax.rsqrt(spread + eps_norm)
    return centred * inverse, inverse


def _dot(a, b, ca=1, cb=0):
    return lax.dot_general(
        a, b, (((ca,), (cb,)), ((), ())), preferred_element_type=jnp.float32
    )


def fused_kernel(
    fields, logit, w_qkv, w_proj, w_merge, w_up, w_down, cot,
    coarse, gcoarse, lvl_o, hid_o, slo_o, spre_o,
    sendq, winq, mixw, mixq, wm, up, down, lvl, hid, dgel, bsend, brecv, slo, spre, gsend, grecv,
    loc, s_q, r_q, s_b, r_b, s_w, r_w, s_l, r_l, s_d, r_d, s_s, r_s, s_g, r_g, s_p, r_p,
):
    f32, bf16 = jnp.float32, jnp.bfloat16
    i, j = lax.axis_index("rows"), lax.axis_index("cols")
    ni, nj = lax.axis_size("rows"), lax.axis_size("cols")
    z = lax.axis_index("dp")
    beside = z + 1 - 2 * (z % 2)
    half_side = WIN // 2
    quad = half_side * half_side
    ch = fields.shape[-1]
    c4 = cot.shape[-1]
    own = cot.shape[0]
    half = c4 // ni
    heads = logit.shape[0]
    width = ch // heads
    other = (i + 1) % ni
    prev_j, next_j = (j + nj - 1) % nj, (j + 1) % nj
    partner = j + 1 - 2 * (j % 2)
    far = (j + 2) % nj
    far_partner = (partner + 2) % nj
    peers = (partner, far, far_partner)

    def remote(src, dst, send, recv, row, col, part=z):
        return pltpu.make_async_remote_copy(
            src_ref=src, dst_ref=dst, send_sem=send, recv_sem=recv,
            device_id={"rows": row, "cols": col, "dp": part},
            device_id_type=pl.DeviceIdType.MESH,
        )

    def quarter(a, b):
        part = fields[a * half_side:(a + 1) * half_side, b * half_side:(b + 1) * half_side, :]
        return part.reshape(quad, ch)

    for k in range(3):
        sendq[k] = quarter(k // 2, k % 2).astype(bf16)
    winq[3] = quarter(1, 1).astype(bf16)

    barrier = pltpu.get_barrier_semaphore()
    greet = [(i, p) for p in peers] + [(other, j), (other, prev_j), (other, next_j)]
    for row, col in greet:
        pl.semaphore_signal(
            barrier, inc=1, device_id={"rows": row, "cols": col},
            device_id_type=pl.DeviceIdType.MESH,
        )
    pl.semaphore_signal(
        barrier, inc=1, device_id={"dp": beside}, device_id_type=pl.DeviceIdType.MESH
    )
    pl.semaphore_wait(barrier, len(greet) + 1)

    targets = ((other, prev_j), (other, j), (i, prev_j))
    backs = ((other, next_j), (other, j), (i, next_j))
    quads = [
        remote(sendq.at[k], winq.at[k], s_q.at[k], r_q.at[k], *targets[k]) for k in range(3)
    ]
    for c in quads:
        c.start()
    ff = w_up.shape[1]
    share, wide = w_merge.shape
    bit = z % 2

    def shard(col):
        return pl.ds(pl.multiple_of(col * share, 64), share)

    def up_half(row, which):
        return pl.ds(pl.multiple_of(row * half + which * (half // 2), half // 2), half // 2)

    def down_half(which):
        return pl.ds(pl.multiple_of(which * (ff // 2), ff // 2), ff // 2)

    def from_half(which):
        return pl.ds(pl.multiple_of(which * (half // 2), half // 2), half // 2)

    merge_out = [
        remote(w_merge, wm.at[shard(j), :], s_w.at[0], r_w.at[0], i, far),
        remote(w_merge, wm.at[shard(j), :], s_w.at[1], r_w.at[1], i, partner),
    ]
    weights_out = [
        remote(w_up.at[from_half(bit), :], up.at[up_half(i, bit), :], s_w.at[2], r_w.at[2], other, j),
        remote(
            w_down.at[down_half(bit), :], down.at[i, down_half(bit), :],
            s_w.at[3], r_w.at[3], other, j,
        ),
    ]
    for c in merge_out + weights_out:
        c.start()
    locals_ = [
        pltpu.make_async_copy(w_merge, wm.at[shard(j), :], loc.at[0]),
        pltpu.make_async_copy(w_up, up.at[pl.ds(pl.multiple_of(i * half, half), half), :], loc.at[1]),
        pltpu.make_async_copy(w_down, down.at[i], loc.at[2]),
    ]
    for c in locals_:
        c.start()

    lane = lax.broadcasted_iota(jnp.int32, (ch, ch), 0) // width
    lane_t = lax.broadcasted_iota(jnp.int32, (ch, ch), 1) // width
    block_ones = (lane == lane_t).astype(f32).astype(bf16)

    def unit(value):
        squares = value * value
        top = squares.astype(bf16)
        low = (squares - top.astype(f32)).astype(bf16)
        total = _dot(top, block_ones) + _dot(low, block_ones)
        return (value * lax.rsqrt(total + eps_unit)).astype(bf16)

    for c in quads:
        c.wait_recv()
    tokens = winq[...].reshape(4 * quad, ch)
    qhat = unit(_dot(tokens, w_qkv[:, :ch]))
    khat = unit(_dot(tokens, w_qkv[:, ch:2 * ch]))
    vals = _dot(tokens, w_qkv[:, 2 * ch:]).astype(bf16)
    per = 128 // width
    lanes = lax.broadcasted_iota(jnp.int32, (4 * quad, 128), 1) // width
    for b in range(ch // 128):
        cut = slice(b * 128, (b + 1) * 128)
        qb, kb, vb = qhat[:, cut], khat[:, cut], vals[:, cut]
        acc = None
        for t in range(per):
            mine = lanes == t
            zero = jnp.zeros_like(qb)
            scores = _dot(jnp.where(mine, qb, zero), kb, 1, 1) * logit[b * per + t]
            weights = jnp.exp(scores)
            weights = (weights / jnp.sum(weights, axis=-1, keepdims=True)).astype(bf16)
            term = _dot(weights, jnp.where(mine, vb, zero))
            acc = term if acc is None else acc + term
        mixw[:, :, cut] = acc.astype(bf16).reshape(4, quad, 128)
    returns = [
        remote(mixw.at[k], mixq.at[k], s_b.at[k], r_b.at[k], *backs[k]) for k in range(3)
    ]
    for c in returns:
        c.start()
    mixq[3] = mixw[3]
    merge_out[0].wait_recv()
    onward = remote(wm.at[shard(far), :], wm.at[shard(far), :], s_w.at[4], r_w.at[4], i, partner)
    onward.start()
    weights_out[0].wait_recv()
    up_on = remote(
        up.at[up_half(other, bit), :], up.at[up_half(other, bit), :],
        s_w.at[5], r_w.at[5], i, j, beside,
    )
    up_on.start()
    rows_out = lax.broadcasted_iota(jnp.int32, (4 * quad, 4 * quad), 0)
    cols_in = lax.broadcasted_iota(jnp.int32, (4 * quad, 4 * quad), 1)
    which, place = rows_out // quad, rows_out % quad
    r = 2 * (place // half_side) + which % 2
    c = 2 * (place % half_side) + which // 2
    source = ((r // half_side) * 2 + c // half_side) * quad + (r % half_side) * half_side + c % half_side
    permute = (source == cols_in).astype(f32).astype(bf16)
    for cp in returns:
        cp.wait_recv()
    normed, _ = _ln(_dot(mixq[...].reshape(4 * quad, ch), w_proj[...]))
    flat = jnp.concatenate([quarter(k // 2, k % 2) for k in range(4)], axis=0)
    stream = (flat + normed).astype(bf16)
    picked = _dot(permute, stream).astype(bf16)
    merged = jnp.concatenate([picked[k * quad:(k + 1) * quad] for k in range(4)], axis=1)
    locals_[0].wait()
    merge_out[1].wait_recv()
    onward.wait_recv()
    projected = _dot(merged, wm[...], 1, 1)
    level, _ = _ln(projected)
    lvl[j] = level.astype(bf16)
    back_half = pl.ds(pl.multiple_of(other * half, 128), half)
    my_half = pl.ds(pl.multiple_of(i * half, 128), half)

    class Gathered:
        def __init__(self, ref, out, send, recv, p_send, p_recv, base):
            self.ref, self.out, self.send, self.recv = ref, out, send, recv
            self.p_send, self.p_recv, self.base = p_send, p_recv, base
            self.out_far = remote(ref.at[j], ref.at[j], send.at[0], recv.at[0], i, far)
            self.out_partner = remote(ref.at[j], ref.at[j], send.at[1], recv.at[1], i, partner)
            self.onward = remote(ref.at[far], ref.at[far], send.at[2], recv.at[2], i, partner)
            self.across = [
                remote(
                    ref.at[s, :, back_half], out.at[1, s],
                    p_send.at[base + k], p_recv.at[base + k], other, j,
                )
                for k, s in enumerate((j, far))
            ]
            self.across_on = [
                remote(
                    out.at[1, s], out.at[1, s],
                    p_send.at[base + 2 + k], p_recv.at[base + 2 + k], i, partner,
                )
                for k, s in enumerate((j, far))
            ]

        def start(self):
            self.out_far.start()
            self.out_partner.start()
            self.across[0].start()

        def relay(self):
            self.out_far.wait_recv()
            self.onward.start()
            self.across[1].start()

        def relay_across(self):
            for k in range(2):
                self.across[k].wait_recv()
                self.across_on[k].start()

        def all(self):
            return [self.out_far, self.out_partner, self.onward] + self.across + self.across_on

    levels = Gathered(lvl, lvl_o, s_l, r_l, s_p, r_p, 0)
    levels.start()
    weights_out[1].wait_recv()
    down_on = remote(
        down.at[other, down_half(bit), :], down.at[other, down_half(bit), :],
        s_w.at[6], r_w.at[6], i, j, beside,
    )
    down_on.start()
    locals_[1].wait()
    locals_[2].wait()
    up_on.wait_recv()

    pair = j // 2
    pairs = (pair, (pair + 1) % 2)

    def rows_of(p):
        return pl.ds(pl.multiple_of(p * 2 * own, 128), 2 * own)

    branch_out, across = [], []
    own_rows = None
    for t in range(2):
        p = pairs[t]
        if t == 0:
            levels.out_partner.wait_recv()
        else:
            levels.onward.wait_recv()
        pre = _dot(lvl[pl.ds(p * 2, 2)].reshape(2 * own, c4), up[...])
        cdf = 0.5 * (1.0 + lax.erf(pre * np.float32(np.sqrt(0.5))))
        hidden = (pre * cdf).astype(bf16)
        hid[rows_of(p), :] = hidden
        dgel[rows_of(p), :] = cdf + pre * (jnp.exp(-0.5 * pre * pre) * np.float32(1 / np.sqrt(2 * np.pi)))
        if t == 0:
            levels.relay()
            down_on.wait_recv()
        out = jnp.concatenate([_dot(hidden, down[k]) for k in range(ni)], axis=1)
        bsend[pl.ds(p * 2, 2)] = out.astype(bf16).reshape(2, own, c4)
        for k in ((0,) if t == 0 else (1, 2)):
            cp = remote(bsend.at[peers[k]], brecv.at[j], s_d.at[k], r_d.at[k], i, peers[k])
            cp.start()
            branch_out.append(cp)
        cp = remote(
            hid.at[rows_of(p), :], hid_o.at[1, rows_of(p), :], s_p.at[8 + t], r_p.at[8 + t], other, j
        )
        cp.start()
        across.append(cp)
    keep = [
        pltpu.make_async_copy(lvl.at[:, :, my_half], lvl_o.at[0], loc.at[3]),
        pltpu.make_async_copy(hid, hid_o.at[0], loc.at[4]),
    ]
    for cp in keep:
        cp.start()
    total = bsend[j].astype(f32)
    for k in range(3):
        branch_out[k].wait_recv()
        total = total + brecv[peers[k]].astype(f32)
    norm, inverse = _ln(total)
    coarse[...] = level + norm
    g = cot[...].astype(f32)
    slope = inverse * (
        g - jnp.mean(g, axis=-1, keepdims=True) - norm * jnp.mean(g * norm, axis=-1, keepdims=True)
    )
    slo[j] = slope.astype(bf16)
    slopes = Gathered(slo, slo_o, s_s, r_s, s_p, r_p, 4)
    slopes.start()
    levels.relay_across()
    grad_out = []
    for t in range(2):
        p = pairs[t]
        if t == 0:
            slopes.out_partner.wait_recv()
        else:
            slopes.onward.wait_recv()
        so = slo[pl.ds(p * 2, 2)].reshape(2 * own, c4)
        back = _dot(so[:, :half], down[0], 1, 1)
        for k in range(1, ni):
            back = back + _dot(so[:, k * half:(k + 1) * half], down[k], 1, 1)
        sp = (dgel[rows_of(p), :] * back).astype(bf16)
        spre[rows_of(p), :] = sp
        if t == 0:
            slopes.relay()
        cp = remote(
            spre.at[rows_of(p), :], spre_o.at[1, rows_of(p), :],
            s_p.at[10 + t], r_p.at[10 + t], other, j,
        )
        cp.start()
        across.append(cp)
        out = _dot(sp, up[...], 1, 1)
        gsend[pl.ds(p * 2, 2)] = out.astype(bf16).reshape(2, own, c4)
        for k in ((0,) if t == 0 else (1, 2)):
            cp = remote(gsend.at[peers[k]], grecv.at[j], s_g.at[k], r_g.at[k], i, peers[k])
            cp.start()
            grad_out.append(cp)
    keep += [
        pltpu.make_async_copy(slo.at[:, :, my_half], slo_o.at[0], loc.at[5]),
        pltpu.make_async_copy(spre, spre_o.at[0], loc.at[6]),
    ]
    keep[2].start()
    keep[3].start()
    slopes.relay_across()
    total = gsend[j].astype(f32)
    for k in range(3):
        grad_out[k].wait_recv()
        total = total + grecv[peers[k]].astype(f32)
    gcoarse[...] = g + total
    for cp in levels.across_on + slopes.across_on + across:
        cp.wait_recv()
    for cp in keep:
        cp.wait()
    sent = quads + merge_out + weights_out + returns + [onward, up_on, down_on]
    for cp in sent + levels.all() + branch_out + slopes.all() + grad_out + across:
        cp.wait_send()


def weight_kernel(coarse_in, gcoarse_in, lvl, hid, slo, spre, coarse, gcoarse, gup, gdown):
    coarse[...] = coarse_in[...]
    gcoarse[...] = gcoarse_in[...]
    gup[...] = _dot(lvl[...], spre[...], 0, 0)
    gdown[...] = _dot(hid[...], slo[...], 0, 0)


def fused(fields, logit_scale, w_qkv, w_proj, w_merge, w_up, w_down, cotangent):
    tile_rows, tile_cols, ch = fields.shape
    ni, nj = lax.axis_size("rows"), lax.axis_size("cols")
    own = cotangent.shape[0] * cotangent.shape[1]
    c4 = cotangent.shape[-1]
    half, ff = w_up.shape
    f32, bf16 = jnp.float32, jnp.bfloat16
    quad = (WIN // 2) ** 2
    vm = pl.BlockSpec(memory_space=pltpu.VMEM)
    hb = pl.BlockSpec(memory_space=pl.ANY)
    dma = pltpu.SemaphoreType.DMA
    band = nj * own
    acts = (
        jax.ShapeDtypeStruct((ni, nj, own, half), bf16),
        jax.ShapeDtypeStruct((ni, band, ff), bf16),
        jax.ShapeDtypeStruct((ni, nj, own, half), bf16),
        jax.ShapeDtypeStruct((ni, band, ff), bf16),
    )
    grid = (jax.ShapeDtypeStruct((own, c4), f32),) * 2
    outs = pl.pallas_call(
        fused_kernel,
        out_shape=grid + acts,
        in_specs=[vm, pl.BlockSpec(memory_space=pltpu.SMEM), vm, vm, hb, hb, hb, vm],
        out_specs=(vm, vm, hb, hb, hb, hb),
        scratch_shapes=[
            pltpu.VMEM((3, quad, ch), bf16),
            pltpu.VMEM((4, quad, ch), bf16),
            pltpu.VMEM((4, quad, ch), bf16),
            pltpu.VMEM((4, quad, ch), bf16),
            pltpu.VMEM((c4, w_merge.shape[0]), bf16),
            pltpu.VMEM((c4, ff), bf16),
            pltpu.VMEM((ni, ff, half), bf16),
            pltpu.VMEM((nj, own, c4), bf16),
            pltpu.VMEM((band, ff), bf16),
            pltpu.VMEM((band, ff), f32),
            pltpu.VMEM((nj, own, c4), bf16),
            pltpu.VMEM((nj, own, c4), bf16),
            pltpu.VMEM((nj, own, c4), bf16),
            pltpu.VMEM((band, ff), bf16),
            pltpu.VMEM((nj, own, c4), bf16),
            pltpu.VMEM((nj, own, c4), bf16),
            dma((7,)),
            dma((3,)), dma((3,)), dma((3,)), dma((3,)), dma((7,)), dma((7,)),
            dma((3,)), dma((3,)), dma((3,)), dma((3,)), dma((3,)), dma((3,)),
            dma((3,)), dma((3,)), dma((12,)), dma((12,)),
        ],
        compiler_params=pltpu.CompilerParams(collective_id=0, has_side_effects=True),
    )(fields, logit_scale, w_qkv, w_proj, w_merge.T, w_up, w_down, cotangent.reshape(own, c4))
    tokens = ni * band
    flat = (
        outs[0], outs[1], outs[2].reshape(tokens, half), outs[3].reshape(tokens, ff),
        outs[4].reshape(tokens, half), outs[5].reshape(tokens, ff),
    )
    outs = pl.pallas_call(
        weight_kernel,
        out_shape=grid
        + (jax.ShapeDtypeStruct((half, ff), f32), jax.ShapeDtypeStruct((ff, half), f32)),
        in_specs=[vm] * 6,
        out_specs=(vm,) * 4,
    )(*flat)
    shape = (tile_rows // 2, tile_cols // 2, c4)
    return outs[0].reshape(shape), outs[1].reshape(shape), outs[2], outs[3]


def device_body(*args):
    fields, _, w_qkv, _, w_merge, w_up, w_down, _ = args
    fits = (
        lax.axis_size("rows") == 2
        and lax.axis_size("cols") == 4
        and lax.axis_size("dp") % 2 == 0
        and fields.shape[:2] == (WIN, WIN)
        and w_up.shape[0] % 128 == 0
        and fields.shape[-1] % 128 == 0
    )
    return fused(*args) if fits else local(*args)


def solution(mesh):
    return jax.shard_map(
        device_body,
        mesh=mesh,
        in_specs=(
            P(("dp", "rows"), "cols", None),
            P(),
            P(),
            P(),
            P(None, "cols"),
            P("rows", "cols"),
            P("cols", "rows"),
            P(("dp", "rows"), "cols", None),
        ),
        out_specs=(
            P(("dp", "rows"), "cols", None),
            P(("dp", "rows"), "cols", None),
            P("rows", ("dp", "cols")),
            P("cols", ("dp", "rows")),
        ),
        check_vma=False,
    )
```

```python
import jax
import jax.numpy as jnp
import numpy as np
from jax import lax
from jax.experimental import pallas as pl
from jax.experimental.pallas import tpu as pltpu
from jax.sharding import PartitionSpec as P

WIN = 16


eps_norm = 1e-05
eps_unit = 1e-06


def padded_2(cells, sides, width):
    for axis, dim in sides:
        count = lax.axis_size(axis)
        head = lax.slice_in_dim(cells, 0, width, axis=dim)
        tail = lax.slice_in_dim(cells, cells.shape[dim] - width, cells.shape[dim], axis=dim)
        cells = jnp.concatenate(
            [
                lax.ppermute(tail, axis, [(i, (i + 1) % count) for i in range(count)]),
                cells,
                lax.ppermute(head, axis, [((i + 1) % count, i) for i in range(count)]),
            ],
            axis=dim,
        )
    return cells


def layer_norm(value):
    average = jnp.mean(value, axis=-1, keepdims=True)
    centred = value - average
    spread = jnp.mean(centred * centred, axis=-1, keepdims=True)
    inverse = lax.rsqrt(spread + eps_norm)
    return (centred * inverse, inverse)


def norm_slope(upstream, normed, inverse):
    first_mean = jnp.mean(upstream, axis=-1, keepdims=True)
    second_mean = jnp.mean(upstream * normed, axis=-1, keepdims=True)
    return inverse * (upstream - first_mean - normed * second_mean)


def unit_heads(value, head_count):
    shaped = value.reshape(value.shape[:-1] + (head_count, value.shape[-1] // head_count))
    squares = jnp.sum(shaped * shaped, axis=-1, keepdims=True)
    return (shaped * lax.rsqrt(squares + eps_unit)).reshape(value.shape)


def windows_of(field_grid, window):
    grid_rows, grid_cols, channels = field_grid.shape
    shaped = field_grid.reshape(grid_rows // window, window, grid_cols // window, window, channels)
    return shaped.transpose(0, 2, 1, 3, 4).reshape(-1, window * window, channels)


def grid_of(blocks, grid_rows, grid_cols, window):
    channels = blocks.shape[-1]
    shaped = blocks.reshape(grid_rows // window, grid_cols // window, window, window, channels)
    return shaped.transpose(0, 2, 1, 3, 4).reshape(grid_rows, grid_cols, channels)


def attend(queries, key_rows, value_rows, logit_scale, head_count):
    number, window_size, channels = queries.shape
    width_head = channels // head_count
    query_heads = queries.reshape(number, window_size, head_count, width_head)
    key_heads = key_rows.reshape(number, window_size, head_count, width_head)
    value_heads = value_rows.reshape(number, window_size, head_count, width_head)
    scores = jnp.einsum(
        "wqhd,wkhd->whqk", query_heads, key_heads, preferred_element_type=jnp.float32
    )
    weights = jnp.exp(scores * logit_scale[None, :, None, None])
    weights = (weights / jnp.sum(weights, axis=-1, keepdims=True)).astype(jnp.bfloat16)
    mixed_out = jnp.einsum(
        "whqk,wkhd->wqhd", weights, value_heads, preferred_element_type=jnp.float32
    )
    return mixed_out.reshape(number, window_size, channels)


def merge_patches(field_grid):
    quarters = (
        field_grid[0::2, 0::2],
        field_grid[1::2, 0::2],
        field_grid[0::2, 1::2],
        field_grid[1::2, 1::2],
    )
    return jnp.concatenate(quarters, axis=-1)


def exact_gelu(value):
    return jax.nn.gelu(value, approximate=False)


def local(fields, logit_scale, w_qkv, w_proj, w_merge, w_up, w_down, cotangent):
    tile_rows, tile_cols, channels = fields.shape
    offset = WIN // 2
    head_count = logit_scale.shape[0]
    tokens = fields.astype(jnp.bfloat16)
    token_rows = tokens.reshape(-1, channels)
    wide_rows = tile_rows + WIN
    wide_cols = tile_cols + WIN
    widened = padded_2(tokens, (("rows", 0), ("cols", 1)), offset)
    wide_proj = jnp.dot(
        widened.reshape(-1, channels), w_qkv[:, channels:], preferred_element_type=jnp.float32
    )
    key_grid = unit_heads(wide_proj[:, :channels], head_count).astype(jnp.bfloat16)
    value_grid = wide_proj[:, channels:].astype(jnp.bfloat16)
    query_raw = jnp.dot(token_rows, w_qkv[:, :channels], preferred_element_type=jnp.float32)
    queries = (
        unit_heads(query_raw, head_count)
        .astype(jnp.bfloat16)
        .reshape(tile_rows, tile_cols, channels)
    )
    padded = jnp.pad(queries, ((offset, offset), (offset, offset), (0, 0)))
    key_blocks = windows_of(key_grid.reshape(wide_rows, wide_cols, channels), WIN)
    value_blocks = windows_of(value_grid.reshape(wide_rows, wide_cols, channels), WIN)
    mixed = attend(windows_of(padded, WIN), key_blocks, value_blocks, logit_scale, head_count)
    mixed = grid_of(mixed, wide_rows, wide_cols, WIN)[
        offset : offset + tile_rows, offset : offset + tile_cols
    ]
    mixed = mixed.astype(jnp.bfloat16).reshape(-1, channels)
    normed, _ = layer_norm(jnp.dot(mixed, w_proj, preferred_element_type=jnp.float32))
    stream = fields + normed.reshape(fields.shape)
    merged = merge_patches(stream).astype(jnp.bfloat16)
    merged_rows = merged.reshape(-1, merged.shape[-1])
    own_count = merged_rows.shape[0]
    partial_band = jnp.dot(
        lax.all_gather(merged_rows, "cols", axis=0, tiled=True),
        w_merge,
        preferred_element_type=jnp.float32,
    )
    projected_band = lax.all_gather(
        partial_band.astype(jnp.bfloat16), "cols", axis=1, tiled=True
    ).astype(partial_band.dtype)
    level_band, _ = layer_norm(projected_band)
    level_b = level_band.astype(jnp.bfloat16)
    level_own = lax.dynamic_slice_in_dim(
        level_band, lax.axis_index("cols") * own_count, own_count, 0
    )
    up_full = lax.all_gather(w_up, "rows", axis=0, tiled=True)
    down_full = lax.all_gather(w_down, "rows", axis=1, tiled=True)
    hidden_pre = jnp.dot(level_b, up_full, preferred_element_type=jnp.float32)
    hidden = exact_gelu(hidden_pre).astype(jnp.bfloat16)
    rows_part = hidden
    branch_out = lax.psum_scatter(
        jnp.dot(rows_part, down_full, preferred_element_type=jnp.float32).astype(jnp.bfloat16),
        "cols",
        scatter_dimension=0,
        tiled=True,
    ).astype(jnp.float32)
    branch_norm, branch_inv = layer_norm(branch_out)
    coarse = level_own + branch_norm
    upstream = cotangent.astype(jnp.float32).reshape(own_count, -1)
    slope_own = norm_slope(upstream, branch_norm, branch_inv).astype(jnp.bfloat16)
    slope_out = lax.all_gather(slope_own, "cols", axis=0, tiled=True)
    slope_hidden = jnp.einsum("tc,fc->tf", slope_out, down_full, preferred_element_type=jnp.float32)
    _, pullback = jax.vjp(exact_gelu, hidden_pre)
    slope_pre = pullback(slope_hidden)[0].astype(jnp.bfloat16)
    rows_part = slope_pre
    slope_input = lax.psum_scatter(
        jnp.einsum("tf,cf->tc", rows_part, up_full, preferred_element_type=jnp.float32).astype(
            jnp.bfloat16
        ),
        "cols",
        scatter_dimension=0,
        tiled=True,
    ).astype(jnp.float32)
    grad_coarse = upstream + slope_input
    term_up = jnp.einsum("tc,tf->cf", level_b, slope_pre, preferred_element_type=jnp.float32)
    term_down = jnp.einsum("tf,tc->fc", hidden, slope_out, preferred_element_type=jnp.float32)
    grad_up, grad_down = (
        lax.psum_scatter(
            term_up.astype(jnp.bfloat16), "rows", scatter_dimension=0, tiled=True
        ).astype(jnp.float32),
        lax.psum_scatter(
            term_down.astype(jnp.bfloat16), "rows", scatter_dimension=1, tiled=True
        ).astype(jnp.float32),
    )
    coarse_shape = (tile_rows // 2, tile_cols // 2, coarse.shape[-1])
    return (coarse.reshape(coarse_shape), grad_coarse.reshape(coarse_shape), grad_up, grad_down)


def _ln(value):
    average = jnp.mean(value, axis=-1, keepdims=True)
    centred = value - average
    spread = jnp.mean(centred * centred, axis=-1, keepdims=True)
    inverse = lax.rsqrt(spread + eps_norm)
    return centred * inverse, inverse


def _dot(a, b, ca=1, cb=0):
    return lax.dot_general(
        a, b, (((ca,), (cb,)), ((), ())), preferred_element_type=jnp.float32
    )


def fused_kernel(
    fields, logit, w_qkv, w_proj, w_merge, w_up, w_down, cot,
    coarse, gcoarse, lvl_o, hid_o, slo_o, spre_o,
    sendq, winq, mixw, mixq, wm, up, down, lvl, hid, dgel, bsend, brecv, slo, spre, gsend, grecv,
    loc, s_q, r_q, s_b, r_b, s_w, r_w, s_l, r_l, s_d, r_d, s_s, r_s, s_g, r_g, s_p, r_p,
):
    f32, bf16 = jnp.float32, jnp.bfloat16
    i, j = lax.axis_index("rows"), lax.axis_index("cols")
    ni, nj = lax.axis_size("rows"), lax.axis_size("cols")
    z = lax.axis_index("dp")
    beside = z + 1 - 2 * (z % 2)
    half_side = WIN // 2
    quad = half_side * half_side
    ch = fields.shape[-1]
    c4 = cot.shape[-1]
    own = cot.shape[0]
    half = c4 // ni
    heads = logit.shape[0]
    width = ch // heads
    other = (i + 1) % ni
    prev_j, next_j = (j + nj - 1) % nj, (j + 1) % nj
    partner = j + 1 - 2 * (j % 2)
    far = (j + 2) % nj
    far_partner = (partner + 2) % nj
    peers = (partner, far, far_partner)

    def remote(src, dst, send, recv, row, col, part=z):
        return pltpu.make_async_remote_copy(
            src_ref=src, dst_ref=dst, send_sem=send, recv_sem=recv,
            device_id={"rows": row, "cols": col, "dp": part},
            device_id_type=pl.DeviceIdType.MESH,
        )

    def quarter(a, b):
        part = fields[a * half_side:(a + 1) * half_side, b * half_side:(b + 1) * half_side, :]
        return part.reshape(quad, ch)

    for k in range(3):
        sendq[k] = quarter(k // 2, k % 2).astype(bf16)
    winq[3] = quarter(1, 1).astype(bf16)

    barrier = pltpu.get_barrier_semaphore()
    greet = [(i, p) for p in peers] + [(other, j), (other, prev_j), (other, next_j)]
    for row, col in greet:
        pl.semaphore_signal(
            barrier, inc=1, device_id={"rows": row, "cols": col},
            device_id_type=pl.DeviceIdType.MESH,
        )
    pl.semaphore_signal(
        barrier, inc=1, device_id={"dp": beside}, device_id_type=pl.DeviceIdType.MESH
    )
    pl.semaphore_wait(barrier, len(greet) + 1)

    targets = ((other, prev_j), (other, j), (i, prev_j))
    backs = ((other, next_j), (other, j), (i, next_j))
    quads = [
        remote(sendq.at[k], winq.at[k], s_q.at[k], r_q.at[k], *targets[k]) for k in range(3)
    ]
    for c in quads:
        c.start()
    ff = w_up.shape[1]
    share, wide = w_merge.shape
    bit = z % 2

    def shard(col):
        return pl.ds(pl.multiple_of(col * share, 64), share)

    def piece(start, size, part):
        return pl.ds(pl.multiple_of(start + part * (size // 2), size // 2), size // 2)

    def up_rows(row, part):
        return piece(row * half + bit * (half // 2), half // 2, part)

    def down_rows(part):
        return piece(bit * (ff // 2), ff // 2, part)

    def merge_rows(col, part):
        return piece(col * share, share, part)

    merge_far = [
        remote(
            w_merge.at[piece(0, share, q), :], wm.at[merge_rows(j, q), :],
            s_w.at[q], r_w.at[q], i, far,
        )
        for q in range(2)
    ]
    merge_on = [
        remote(
            wm.at[merge_rows(far, q), :], wm.at[merge_rows(far, q), :],
            s_w.at[2 + q], r_w.at[2 + q], i, partner,
        )
        for q in range(2)
    ]
    merge_beside = remote(w_merge, wm.at[shard(j), :], s_w.at[4], r_w.at[4], i, partner)
    up_out = [
        remote(
            w_up.at[up_rows(0, q), :], up.at[up_rows(i, q), :], s_w.at[5 + q], r_w.at[5 + q], other, j
        )
        for q in range(2)
    ]
    up_on = [
        remote(
            up.at[up_rows(other, q), :], up.at[up_rows(other, q), :],
            s_w.at[7 + q], r_w.at[7 + q], i, j, beside,
        )
        for q in range(2)
    ]
    down_out = [
        remote(
            w_down.at[down_rows(q), :], down.at[i, down_rows(q), :],
            s_w.at[9 + q], r_w.at[9 + q], other, j,
        )
        for q in range(2)
    ]
    down_on = [
        remote(
            down.at[other, down_rows(q), :], down.at[other, down_rows(q), :],
            s_w.at[11 + q], r_w.at[11 + q], i, j, beside,
        )
        for q in range(2)
    ]
    for c in (up_out[0], merge_far[0], merge_beside, up_out[1]):
        c.start()
    locals_ = [
        pltpu.make_async_copy(w_merge, wm.at[shard(j), :], loc.at[0]),
        pltpu.make_async_copy(w_up, up.at[pl.ds(pl.multiple_of(i * half, half), half), :], loc.at[1]),
        pltpu.make_async_copy(w_down, down.at[i], loc.at[2]),
    ]
    for c in locals_:
        c.start()

    lane = lax.broadcasted_iota(jnp.int32, (ch, ch), 0) // width
    lane_t = lax.broadcasted_iota(jnp.int32, (ch, ch), 1) // width
    block_ones = (lane == lane_t).astype(f32).astype(bf16)

    def unit(value):
        squares = value * value
        top = squares.astype(bf16)
        low = (squares - top.astype(f32)).astype(bf16)
        total = _dot(top, block_ones) + _dot(low, block_ones)
        return (value * lax.rsqrt(total + eps_unit)).astype(bf16)

    for c in quads:
        c.wait_recv()
    tokens = winq[...].reshape(4 * quad, ch)
    qhat = unit(_dot(tokens, w_qkv[:, :ch]))
    khat = unit(_dot(tokens, w_qkv[:, ch:2 * ch]))
    vals = _dot(tokens, w_qkv[:, 2 * ch:]).astype(bf16)
    up_out[0].wait_recv()
    up_on[0].start()
    per = 128 // width
    lanes = lax.broadcasted_iota(jnp.int32, (4 * quad, 128), 1) // width
    for b in range(ch // 128):
        cut = slice(b * 128, (b + 1) * 128)
        qb, kb, vb = qhat[:, cut], khat[:, cut], vals[:, cut]
        acc = None
        for t in range(per):
            mine = lanes == t
            zero = jnp.zeros_like(qb)
            scores = _dot(jnp.where(mine, qb, zero), kb, 1, 1) * logit[b * per + t]
            weights = jnp.exp(scores)
            weights = (weights / jnp.sum(weights, axis=-1, keepdims=True)).astype(bf16)
            term = _dot(weights, jnp.where(mine, vb, zero))
            acc = term if acc is None else acc + term
        mixw[:, :, cut] = acc.astype(bf16).reshape(4, quad, 128)
    returns = [
        remote(mixw.at[k], mixq.at[k], s_b.at[k], r_b.at[k], *backs[k]) for k in range(3)
    ]
    for c in returns:
        c.start()
    for c in (merge_far[1], down_out[0], down_out[1]):
        c.start()
    mixq[3] = mixw[3]
    up_out[1].wait_recv()
    up_on[1].start()
    merge_far[0].wait_recv()
    merge_on[0].start()
    rows_out = lax.broadcasted_iota(jnp.int32, (4 * quad, 4 * quad), 0)
    cols_in = lax.broadcasted_iota(jnp.int32, (4 * quad, 4 * quad), 1)
    which, place = rows_out // quad, rows_out % quad
    r = 2 * (place // half_side) + which % 2
    c = 2 * (place % half_side) + which // 2
    source = ((r // half_side) * 2 + c // half_side) * quad + (r % half_side) * half_side + c % half_side
    permute = (source == cols_in).astype(f32).astype(bf16)
    for cp in returns:
        cp.wait_recv()
    normed, _ = _ln(_dot(mixq[...].reshape(4 * quad, ch), w_proj[...]))
    flat = jnp.concatenate([quarter(k // 2, k % 2) for k in range(4)], axis=0)
    stream = (flat + normed).astype(bf16)
    picked = _dot(permute, stream).astype(bf16)
    merged = jnp.concatenate([picked[k * quad:(k + 1) * quad] for k in range(4)], axis=1)
    locals_[0].wait()
    down_out[0].wait_recv()
    down_on[0].start()
    merge_far[1].wait_recv()
    merge_on[1].start()
    for c in (merge_beside, merge_on[0], merge_on[1]):
        c.wait_recv()
    projected = _dot(merged, wm[...], 1, 1)
    level, _ = _ln(projected)
    lvl[j] = level.astype(bf16)
    back_half = pl.ds(pl.multiple_of(other * half, 128), half)
    my_half = pl.ds(pl.multiple_of(i * half, 128), half)

    class Gathered:
        def __init__(self, ref, out, send, recv, p_send, p_recv, base):
            self.ref, self.out, self.send, self.recv = ref, out, send, recv
            self.p_send, self.p_recv, self.base = p_send, p_recv, base
            self.out_far = remote(ref.at[j], ref.at[j], send.at[0], recv.at[0], i, far)
            self.out_partner = remote(ref.at[j], ref.at[j], send.at[1], recv.at[1], i, partner)
            self.onward = remote(ref.at[far], ref.at[far], send.at[2], recv.at[2], i, partner)
            self.across = [
                remote(
                    ref.at[s, :, back_half], out.at[1, s],
                    p_send.at[base + k], p_recv.at[base + k], other, j,
                )
                for k, s in enumerate((j, far))
            ]
            self.across_on = [
                remote(
                    out.at[1, s], out.at[1, s],
                    p_send.at[base + 2 + k], p_recv.at[base + 2 + k], i, partner,
                )
                for k, s in enumerate((j, far))
            ]

        def start(self):
            self.out_far.start()
            self.out_partner.start()
            self.across[0].start()

        def relay(self):
            self.out_far.wait_recv()
            self.onward.start()
            self.across[1].start()

        def relay_across(self):
            for k in range(2):
                self.across[k].wait_recv()
                self.across_on[k].start()

        def all(self):
            return [self.out_far, self.out_partner, self.onward] + self.across + self.across_on

    levels = Gathered(lvl, lvl_o, s_l, r_l, s_p, r_p, 0)
    levels.start()
    down_out[1].wait_recv()
    down_on[1].start()
    locals_[1].wait()
    locals_[2].wait()
    up_on[0].wait_recv()
    up_on[1].wait_recv()

    pair = j // 2
    pairs = (pair, (pair + 1) % 2)

    def rows_of(p):
        return pl.ds(pl.multiple_of(p * 2 * own, 128), 2 * own)

    branch_out, across = [], []
    own_rows = None
    for t in range(2):
        p = pairs[t]
        if t == 0:
            levels.out_partner.wait_recv()
        else:
            levels.onward.wait_recv()
        pre = _dot(lvl[pl.ds(p * 2, 2)].reshape(2 * own, c4), up[...])
        cdf = 0.5 * (1.0 + lax.erf(pre * np.float32(np.sqrt(0.5))))
        hidden = (pre * cdf).astype(bf16)
        hid[rows_of(p), :] = hidden
        dgel[rows_of(p), :] = cdf + pre * (jnp.exp(-0.5 * pre * pre) * np.float32(1 / np.sqrt(2 * np.pi)))
        if t == 0:
            levels.relay()
            down_on[0].wait_recv()
            down_on[1].wait_recv()
        out = jnp.concatenate([_dot(hidden, down[k]) for k in range(ni)], axis=1)
        bsend[pl.ds(p * 2, 2)] = out.astype(bf16).reshape(2, own, c4)
        for k in ((0,) if t == 0 else (1, 2)):
            cp = remote(bsend.at[peers[k]], brecv.at[j], s_d.at[k], r_d.at[k], i, peers[k])
            cp.start()
            branch_out.append(cp)
        cp = remote(
            hid.at[rows_of(p), :], hid_o.at[1, rows_of(p), :], s_p.at[8 + t], r_p.at[8 + t], other, j
        )
        cp.start()
        across.append(cp)
    keep = [
        pltpu.make_async_copy(lvl.at[:, :, my_half], lvl_o.at[0], loc.at[3]),
        pltpu.make_async_copy(hid, hid_o.at[0], loc.at[4]),
    ]
    for cp in keep:
        cp.start()
    total = bsend[j].astype(f32)
    for k in range(3):
        branch_out[k].wait_recv()
        total = total + brecv[peers[k]].astype(f32)
    norm, inverse = _ln(total)
    coarse[...] = level + norm
    g = cot[...].astype(f32)
    slope = inverse * (
        g - jnp.mean(g, axis=-1, keepdims=True) - norm * jnp.mean(g * norm, axis=-1, keepdims=True)
    )
    slo[j] = slope.astype(bf16)
    slopes = Gathered(slo, slo_o, s_s, r_s, s_p, r_p, 4)
    slopes.start()
    levels.relay_across()
    grad_out = []
    for t in range(2):
        p = pairs[t]
        if t == 0:
            slopes.out_partner.wait_recv()
        else:
            slopes.onward.wait_recv()
        so = slo[pl.ds(p * 2, 2)].reshape(2 * own, c4)
        back = _dot(so[:, :half], down[0], 1, 1)
        for k in range(1, ni):
            back = back + _dot(so[:, k * half:(k + 1) * half], down[k], 1, 1)
        sp = (dgel[rows_of(p), :] * back).astype(bf16)
        spre[rows_of(p), :] = sp
        if t == 0:
            slopes.relay()
        cp = remote(
            spre.at[rows_of(p), :], spre_o.at[1, rows_of(p), :],
            s_p.at[10 + t], r_p.at[10 + t], other, j,
        )
        cp.start()
        across.append(cp)
        out = _dot(sp, up[...], 1, 1)
        gsend[pl.ds(p * 2, 2)] = out.astype(bf16).reshape(2, own, c4)
        for k in ((0,) if t == 0 else (1, 2)):
            cp = remote(gsend.at[peers[k]], grecv.at[j], s_g.at[k], r_g.at[k], i, peers[k])
            cp.start()
            grad_out.append(cp)
    keep += [
        pltpu.make_async_copy(slo.at[:, :, my_half], slo_o.at[0], loc.at[5]),
        pltpu.make_async_copy(spre, spre_o.at[0], loc.at[6]),
    ]
    keep[2].start()
    keep[3].start()
    slopes.relay_across()
    total = gsend[j].astype(f32)
    for k in range(3):
        grad_out[k].wait_recv()
        total = total + grecv[peers[k]].astype(f32)
    gcoarse[...] = g + total
    for cp in levels.across_on + slopes.across_on + across:
        cp.wait_recv()
    for cp in keep:
        cp.wait()
    weights = merge_far + merge_on + [merge_beside] + up_out + up_on + down_out + down_on
    sent = quads + weights + returns
    for cp in sent + levels.all() + branch_out + slopes.all() + grad_out + across:
        cp.wait_send()


def weight_kernel(coarse_in, gcoarse_in, lvl, hid, slo, spre, coarse, gcoarse, gup, gdown):
    coarse[...] = coarse_in[...]
    gcoarse[...] = gcoarse_in[...]
    gup[...] = _dot(lvl[...], spre[...], 0, 0)
    gdown[...] = _dot(hid[...], slo[...], 0, 0)


def fused(fields, logit_scale, w_qkv, w_proj, w_merge, w_up, w_down, cotangent):
    tile_rows, tile_cols, ch = fields.shape
    ni, nj = lax.axis_size("rows"), lax.axis_size("cols")
    own = cotangent.shape[0] * cotangent.shape[1]
    c4 = cotangent.shape[-1]
    half, ff = w_up.shape
    f32, bf16 = jnp.float32, jnp.bfloat16
    quad = (WIN // 2) ** 2
    vm = pl.BlockSpec(memory_space=pltpu.VMEM)
    hb = pl.BlockSpec(memory_space=pl.ANY)
    dma = pltpu.SemaphoreType.DMA
    band = nj * own
    acts = (
        jax.ShapeDtypeStruct((ni, nj, own, half), bf16),
        jax.ShapeDtypeStruct((ni, band, ff), bf16),
        jax.ShapeDtypeStruct((ni, nj, own, half), bf16),
        jax.ShapeDtypeStruct((ni, band, ff), bf16),
    )
    grid = (jax.ShapeDtypeStruct((own, c4), f32),) * 2
    outs = pl.pallas_call(
        fused_kernel,
        out_shape=grid + acts,
        in_specs=[vm, pl.BlockSpec(memory_space=pltpu.SMEM), vm, vm, hb, hb, hb, vm],
        out_specs=(vm, vm, hb, hb, hb, hb),
        scratch_shapes=[
            pltpu.VMEM((3, quad, ch), bf16),
            pltpu.VMEM((4, quad, ch), bf16),
            pltpu.VMEM((4, quad, ch), bf16),
            pltpu.VMEM((4, quad, ch), bf16),
            pltpu.VMEM((c4, w_merge.shape[0]), bf16),
            pltpu.VMEM((c4, ff), bf16),
            pltpu.VMEM((ni, ff, half), bf16),
            pltpu.VMEM((nj, own, c4), bf16),
            pltpu.VMEM((band, ff), bf16),
            pltpu.VMEM((band, ff), f32),
            pltpu.VMEM((nj, own, c4), bf16),
            pltpu.VMEM((nj, own, c4), bf16),
            pltpu.VMEM((nj, own, c4), bf16),
            pltpu.VMEM((band, ff), bf16),
            pltpu.VMEM((nj, own, c4), bf16),
            pltpu.VMEM((nj, own, c4), bf16),
            dma((7,)),
            dma((3,)), dma((3,)), dma((3,)), dma((3,)), dma((13,)), dma((13,)),
            dma((3,)), dma((3,)), dma((3,)), dma((3,)), dma((3,)), dma((3,)),
            dma((3,)), dma((3,)), dma((12,)), dma((12,)),
        ],
        compiler_params=pltpu.CompilerParams(collective_id=0, has_side_effects=True),
    )(fields, logit_scale, w_qkv, w_proj, w_merge.T, w_up, w_down, cotangent.reshape(own, c4))
    tokens = ni * band
    flat = (
        outs[0], outs[1], outs[2].reshape(tokens, half), outs[3].reshape(tokens, ff),
        outs[4].reshape(tokens, half), outs[5].reshape(tokens, ff),
    )
    outs = pl.pallas_call(
        weight_kernel,
        out_shape=grid
        + (jax.ShapeDtypeStruct((half, ff), f32), jax.ShapeDtypeStruct((ff, half), f32)),
        in_specs=[vm] * 6,
        out_specs=(vm,) * 4,
    )(*flat)
    shape = (tile_rows // 2, tile_cols // 2, c4)
    return outs[0].reshape(shape), outs[1].reshape(shape), outs[2], outs[3]


def device_body(*args):
    fields, _, w_qkv, _, w_merge, w_up, w_down, _ = args
    fits = (
        lax.axis_size("rows") == 2
        and lax.axis_size("cols") == 4
        and lax.axis_size("dp") % 2 == 0
        and fields.shape[:2] == (WIN, WIN)
        and w_up.shape[0] % 128 == 0
        and fields.shape[-1] % 128 == 0
    )
    return fused(*args) if fits else local(*args)


def solution(mesh):
    return jax.shard_map(
        device_body,
        mesh=mesh,
        in_specs=(
            P(("dp", "rows"), "cols", None),
            P(),
            P(),
            P(),
            P(None, "cols"),
            P("rows", "cols"),
            P("cols", "rows"),
            P(("dp", "rows"), "cols", None),
        ),
        out_specs=(
            P(("dp", "rows"), "cols", None),
            P(("dp", "rows"), "cols", None),
            P("rows", ("dp", "cols")),
            P("cols", ("dp", "rows")),
        ),
        check_vma=False,
    )
```

```python
import jax
import jax.numpy as jnp
import numpy as np
from jax import lax
from jax.experimental import pallas as pl
from jax.experimental.pallas import tpu as pltpu
from jax.sharding import PartitionSpec as P

WIN = 16


eps_norm = 1e-05
eps_unit = 1e-06


def padded_2(cells, sides, width):
    for axis, dim in sides:
        count = lax.axis_size(axis)
        head = lax.slice_in_dim(cells, 0, width, axis=dim)
        tail = lax.slice_in_dim(cells, cells.shape[dim] - width, cells.shape[dim], axis=dim)
        cells = jnp.concatenate(
            [
                lax.ppermute(tail, axis, [(i, (i + 1) % count) for i in range(count)]),
                cells,
                lax.ppermute(head, axis, [((i + 1) % count, i) for i in range(count)]),
            ],
            axis=dim,
        )
    return cells


def layer_norm(value):
    average = jnp.mean(value, axis=-1, keepdims=True)
    centred = value - average
    spread = jnp.mean(centred * centred, axis=-1, keepdims=True)
    inverse = lax.rsqrt(spread + eps_norm)
    return (centred * inverse, inverse)


def norm_slope(upstream, normed, inverse):
    first_mean = jnp.mean(upstream, axis=-1, keepdims=True)
    second_mean = jnp.mean(upstream * normed, axis=-1, keepdims=True)
    return inverse * (upstream - first_mean - normed * second_mean)


def unit_heads(value, head_count):
    shaped = value.reshape(value.shape[:-1] + (head_count, value.shape[-1] // head_count))
    squares = jnp.sum(shaped * shaped, axis=-1, keepdims=True)
    return (shaped * lax.rsqrt(squares + eps_unit)).reshape(value.shape)


def windows_of(field_grid, window):
    grid_rows, grid_cols, channels = field_grid.shape
    shaped = field_grid.reshape(grid_rows // window, window, grid_cols // window, window, channels)
    return shaped.transpose(0, 2, 1, 3, 4).reshape(-1, window * window, channels)


def grid_of(blocks, grid_rows, grid_cols, window):
    channels = blocks.shape[-1]
    shaped = blocks.reshape(grid_rows // window, grid_cols // window, window, window, channels)
    return shaped.transpose(0, 2, 1, 3, 4).reshape(grid_rows, grid_cols, channels)


def attend(queries, key_rows, value_rows, logit_scale, head_count):
    number, window_size, channels = queries.shape
    width_head = channels // head_count
    query_heads = queries.reshape(number, window_size, head_count, width_head)
    key_heads = key_rows.reshape(number, window_size, head_count, width_head)
    value_heads = value_rows.reshape(number, window_size, head_count, width_head)
    scores = jnp.einsum(
        "wqhd,wkhd->whqk", query_heads, key_heads, preferred_element_type=jnp.float32
    )
    weights = jnp.exp(scores * logit_scale[None, :, None, None])
    weights = (weights / jnp.sum(weights, axis=-1, keepdims=True)).astype(jnp.bfloat16)
    mixed_out = jnp.einsum(
        "whqk,wkhd->wqhd", weights, value_heads, preferred_element_type=jnp.float32
    )
    return mixed_out.reshape(number, window_size, channels)


def merge_patches(field_grid):
    quarters = (
        field_grid[0::2, 0::2],
        field_grid[1::2, 0::2],
        field_grid[0::2, 1::2],
        field_grid[1::2, 1::2],
    )
    return jnp.concatenate(quarters, axis=-1)


def exact_gelu(value):
    return jax.nn.gelu(value, approximate=False)


def local(fields, logit_scale, w_qkv, w_proj, w_merge, w_up, w_down, cotangent):
    tile_rows, tile_cols, channels = fields.shape
    offset = WIN // 2
    head_count = logit_scale.shape[0]
    tokens = fields.astype(jnp.bfloat16)
    token_rows = tokens.reshape(-1, channels)
    wide_rows = tile_rows + WIN
    wide_cols = tile_cols + WIN
    widened = padded_2(tokens, (("rows", 0), ("cols", 1)), offset)
    wide_proj = jnp.dot(
        widened.reshape(-1, channels), w_qkv[:, channels:], preferred_element_type=jnp.float32
    )
    key_grid = unit_heads(wide_proj[:, :channels], head_count).astype(jnp.bfloat16)
    value_grid = wide_proj[:, channels:].astype(jnp.bfloat16)
    query_raw = jnp.dot(token_rows, w_qkv[:, :channels], preferred_element_type=jnp.float32)
    queries = (
        unit_heads(query_raw, head_count)
        .astype(jnp.bfloat16)
        .reshape(tile_rows, tile_cols, channels)
    )
    padded = jnp.pad(queries, ((offset, offset), (offset, offset), (0, 0)))
    key_blocks = windows_of(key_grid.reshape(wide_rows, wide_cols, channels), WIN)
    value_blocks = windows_of(value_grid.reshape(wide_rows, wide_cols, channels), WIN)
    mixed = attend(windows_of(padded, WIN), key_blocks, value_blocks, logit_scale, head_count)
    mixed = grid_of(mixed, wide_rows, wide_cols, WIN)[
        offset : offset + tile_rows, offset : offset + tile_cols
    ]
    mixed = mixed.astype(jnp.bfloat16).reshape(-1, channels)
    normed, _ = layer_norm(jnp.dot(mixed, w_proj, preferred_element_type=jnp.float32))
    stream = fields + normed.reshape(fields.shape)
    merged = merge_patches(stream).astype(jnp.bfloat16)
    merged_rows = merged.reshape(-1, merged.shape[-1])
    own_count = merged_rows.shape[0]
    partial_band = jnp.dot(
        lax.all_gather(merged_rows, "cols", axis=0, tiled=True),
        w_merge,
        preferred_element_type=jnp.float32,
    )
    projected_band = lax.all_gather(
        partial_band.astype(jnp.bfloat16), "cols", axis=1, tiled=True
    ).astype(partial_band.dtype)
    level_band, _ = layer_norm(projected_band)
    level_b = level_band.astype(jnp.bfloat16)
    level_own = lax.dynamic_slice_in_dim(
        level_band, lax.axis_index("cols") * own_count, own_count, 0
    )
    up_full = lax.all_gather(w_up, "rows", axis=0, tiled=True)
    down_full = lax.all_gather(w_down, "rows", axis=1, tiled=True)
    hidden_pre = jnp.dot(level_b, up_full, preferred_element_type=jnp.float32)
    hidden = exact_gelu(hidden_pre).astype(jnp.bfloat16)
    rows_part = hidden
    branch_out = lax.psum_scatter(
        jnp.dot(rows_part, down_full, preferred_element_type=jnp.float32).astype(jnp.bfloat16),
        "cols",
        scatter_dimension=0,
        tiled=True,
    ).astype(jnp.float32)
    branch_norm, branch_inv = layer_norm(branch_out)
    coarse = level_own + branch_norm
    upstream = cotangent.astype(jnp.float32).reshape(own_count, -1)
    slope_own = norm_slope(upstream, branch_norm, branch_inv).astype(jnp.bfloat16)
    slope_out = lax.all_gather(slope_own, "cols", axis=0, tiled=True)
    slope_hidden = jnp.einsum("tc,fc->tf", slope_out, down_full, preferred_element_type=jnp.float32)
    _, pullback = jax.vjp(exact_gelu, hidden_pre)
    slope_pre = pullback(slope_hidden)[0].astype(jnp.bfloat16)
    rows_part = slope_pre
    slope_input = lax.psum_scatter(
        jnp.einsum("tf,cf->tc", rows_part, up_full, preferred_element_type=jnp.float32).astype(
            jnp.bfloat16
        ),
        "cols",
        scatter_dimension=0,
        tiled=True,
    ).astype(jnp.float32)
    grad_coarse = upstream + slope_input
    term_up = jnp.einsum("tc,tf->cf", level_b, slope_pre, preferred_element_type=jnp.float32)
    term_down = jnp.einsum("tf,tc->fc", hidden, slope_out, preferred_element_type=jnp.float32)
    grad_up, grad_down = (
        lax.psum_scatter(
            term_up.astype(jnp.bfloat16), "rows", scatter_dimension=0, tiled=True
        ).astype(jnp.float32),
        lax.psum_scatter(
            term_down.astype(jnp.bfloat16), "rows", scatter_dimension=1, tiled=True
        ).astype(jnp.float32),
    )
    coarse_shape = (tile_rows // 2, tile_cols // 2, coarse.shape[-1])
    return (coarse.reshape(coarse_shape), grad_coarse.reshape(coarse_shape), grad_up, grad_down)


def _ln(value):
    average = jnp.mean(value, axis=-1, keepdims=True)
    centred = value - average
    spread = jnp.mean(centred * centred, axis=-1, keepdims=True)
    inverse = lax.rsqrt(spread + eps_norm)
    return centred * inverse, inverse


def _dot(a, b, ca=1, cb=0):
    return lax.dot_general(
        a, b, (((ca,), (cb,)), ((), ())), preferred_element_type=jnp.float32
    )


def fused_kernel(
    fields, logit, w_qkv, w_proj, w_merge, w_up, w_down, cot,
    coarse, gcoarse, lvl_o, hid_o, slo_o, spre_o,
    sendq, winq, mixw, mixq, wm, up, down, lvl, hid, dgel, bsend, brecv, slo, spre, gsend, grecv,
    loc, s_q, r_q, s_b, r_b, s_w, r_w, s_l, r_l, s_d, r_d, s_s, r_s, s_g, r_g, s_p, r_p,
):
    f32, bf16 = jnp.float32, jnp.bfloat16
    i, j = lax.axis_index("rows"), lax.axis_index("cols")
    ni, nj = lax.axis_size("rows"), lax.axis_size("cols")
    z = lax.axis_index("dp")
    beside = z + 1 - 2 * (z % 2)
    half_side = WIN // 2
    quad = half_side * half_side
    ch = fields.shape[-1]
    c4 = cot.shape[-1]
    own = cot.shape[0]
    half = c4 // ni
    heads = logit.shape[0]
    width = ch // heads
    other = (i + 1) % ni
    prev_j, next_j = (j + nj - 1) % nj, (j + 1) % nj
    partner = j + 1 - 2 * (j % 2)
    far = (j + 2) % nj
    far_partner = (partner + 2) % nj
    peers = (partner, far, far_partner)

    def remote(src, dst, send, recv, row, col, part=z):
        return pltpu.make_async_remote_copy(
            src_ref=src, dst_ref=dst, send_sem=send, recv_sem=recv,
            device_id={"rows": row, "cols": col, "dp": part},
            device_id_type=pl.DeviceIdType.MESH,
        )

    def quarter(a, b):
        part = fields[a * half_side:(a + 1) * half_side, b * half_side:(b + 1) * half_side, :]
        return part.reshape(quad, ch)

    for k in range(3):
        sendq[k] = quarter(k // 2, k % 2).astype(bf16)
    winq[3] = quarter(1, 1).astype(bf16)

    barrier = pltpu.get_barrier_semaphore()
    greet = [(i, p) for p in peers] + [(other, j), (other, prev_j), (other, next_j)]
    for row, col in greet:
        pl.semaphore_signal(
            barrier, inc=1, device_id={"rows": row, "cols": col},
            device_id_type=pl.DeviceIdType.MESH,
        )
    pl.semaphore_signal(
        barrier, inc=1, device_id={"dp": beside}, device_id_type=pl.DeviceIdType.MESH
    )
    pl.semaphore_wait(barrier, len(greet) + 1)

    targets = ((other, prev_j), (other, j), (i, prev_j))
    backs = ((other, next_j), (other, j), (i, next_j))
    quads = [
        remote(sendq.at[k], winq.at[k], s_q.at[k], r_q.at[k], *targets[k]) for k in range(3)
    ]
    for c in quads:
        c.start()
    ff = w_up.shape[1]
    share, wide = w_merge.shape
    bit = z % 2

    def shard(col):
        return pl.ds(pl.multiple_of(col * share, 64), share)

    def piece(start, size, part):
        return pl.ds(pl.multiple_of(start + part * (size // 2), size // 2), size // 2)

    def up_rows(row, part):
        return piece(row * half + bit * (half // 2), half // 2, part)

    def down_rows(part):
        return piece(bit * (ff // 2), ff // 2, part)

    def merge_rows(col, part):
        return piece(col * share, share, part)

    merge_far = [
        remote(
            w_merge.at[piece(0, share, q), :], wm.at[merge_rows(j, q), :],
            s_w.at[q], r_w.at[q], i, far,
        )
        for q in range(2)
    ]
    merge_on = [
        remote(
            wm.at[merge_rows(far, q), :], wm.at[merge_rows(far, q), :],
            s_w.at[2 + q], r_w.at[2 + q], i, partner,
        )
        for q in range(2)
    ]
    merge_beside = remote(w_merge, wm.at[shard(j), :], s_w.at[4], r_w.at[4], i, partner)
    up_out = [
        remote(
            w_up.at[up_rows(0, q), :], up.at[up_rows(i, q), :], s_w.at[5 + q], r_w.at[5 + q], other, j
        )
        for q in range(2)
    ]
    up_on = [
        remote(
            up.at[up_rows(other, q), :], up.at[up_rows(other, q), :],
            s_w.at[7 + q], r_w.at[7 + q], i, j, beside,
        )
        for q in range(2)
    ]
    down_out = [
        remote(
            w_down.at[down_rows(q), :], down.at[i, down_rows(q), :],
            s_w.at[9 + q], r_w.at[9 + q], other, j,
        )
        for q in range(2)
    ]
    down_on = [
        remote(
            down.at[other, down_rows(q), :], down.at[other, down_rows(q), :],
            s_w.at[11 + q], r_w.at[11 + q], i, j, beside,
        )
        for q in range(2)
    ]
    for c in (up_out[0], merge_far[0], merge_beside, up_out[1]):
        c.start()
    locals_ = [
        pltpu.make_async_copy(w_merge, wm.at[shard(j), :], loc.at[0]),
        pltpu.make_async_copy(w_up, up.at[pl.ds(pl.multiple_of(i * half, half), half), :], loc.at[1]),
        pltpu.make_async_copy(w_down, down.at[i], loc.at[2]),
    ]
    for c in locals_:
        c.start()

    lane = lax.broadcasted_iota(jnp.int32, (ch, ch), 0) // width
    lane_t = lax.broadcasted_iota(jnp.int32, (ch, ch), 1) // width
    block_ones = (lane == lane_t).astype(f32).astype(bf16)

    def unit(value):
        squares = value * value
        top = squares.astype(bf16)
        low = (squares - top.astype(f32)).astype(bf16)
        total = _dot(top, block_ones) + _dot(low, block_ones)
        return (value * lax.rsqrt(total + eps_unit)).astype(bf16)

    for c in quads:
        c.wait_recv()
    tokens = winq[...].reshape(4 * quad, ch)
    qhat = unit(_dot(tokens, w_qkv[:, :ch]))
    khat = unit(_dot(tokens, w_qkv[:, ch:2 * ch]))
    vals = _dot(tokens, w_qkv[:, 2 * ch:]).astype(bf16)
    up_out[0].wait_recv()
    up_on[0].start()
    per = 128 // width
    lanes = lax.broadcasted_iota(jnp.int32, (4 * quad, 128), 1) // width
    for b in range(ch // 128):
        cut = slice(b * 128, (b + 1) * 128)
        qb, kb, vb = qhat[:, cut], khat[:, cut], vals[:, cut]
        acc = None
        for t in range(per):
            mine = lanes == t
            zero = jnp.zeros_like(qb)
            scores = _dot(jnp.where(mine, qb, zero), kb, 1, 1) * logit[b * per + t]
            weights = jnp.exp(scores)
            weights = (weights / jnp.sum(weights, axis=-1, keepdims=True)).astype(bf16)
            term = _dot(weights, jnp.where(mine, vb, zero))
            acc = term if acc is None else acc + term
        mixw[:, :, cut] = acc.astype(bf16).reshape(4, quad, 128)
    returns = [
        remote(mixw.at[k], mixq.at[k], s_b.at[k], r_b.at[k], *backs[k]) for k in range(3)
    ]
    for c in returns:
        c.start()
    for c in (merge_far[1], down_out[0], down_out[1]):
        c.start()
    mixq[3] = mixw[3]
    up_out[1].wait_recv()
    up_on[1].start()
    merge_far[0].wait_recv()
    merge_on[0].start()
    rows_out = lax.broadcasted_iota(jnp.int32, (4 * quad, 4 * quad), 0)
    cols_in = lax.broadcasted_iota(jnp.int32, (4 * quad, 4 * quad), 1)
    which, place = rows_out // quad, rows_out % quad
    r = 2 * (place // half_side) + which % 2
    c = 2 * (place % half_side) + which // 2
    source = ((r // half_side) * 2 + c // half_side) * quad + (r % half_side) * half_side + c % half_side
    permute = (source == cols_in).astype(f32).astype(bf16)
    for cp in returns:
        cp.wait_recv()
    normed, _ = _ln(_dot(mixq[...].reshape(4 * quad, ch), w_proj[...]))
    flat = jnp.concatenate([quarter(k // 2, k % 2) for k in range(4)], axis=0)
    stream = (flat + normed).astype(bf16)
    picked = _dot(permute, stream).astype(bf16)
    merged = jnp.concatenate([picked[k * quad:(k + 1) * quad] for k in range(4)], axis=1)
    locals_[0].wait()
    down_out[0].wait_recv()
    down_on[0].start()
    merge_far[1].wait_recv()
    merge_on[1].start()
    for c in (merge_beside, merge_on[0], merge_on[1]):
        c.wait_recv()
    projected = _dot(merged, wm[...], 1, 1)
    level, _ = _ln(projected)
    lvl[j] = level.astype(bf16)
    back_half = pl.ds(pl.multiple_of(other * half, 128), half)
    my_half = pl.ds(pl.multiple_of(i * half, 128), half)

    class Gathered:
        def __init__(self, ref, out, send, recv, p_send, p_recv, base):
            self.ref, self.out, self.send, self.recv = ref, out, send, recv
            self.p_send, self.p_recv, self.base = p_send, p_recv, base
            self.out_far = remote(ref.at[j], ref.at[j], send.at[0], recv.at[0], i, far)
            self.out_partner = remote(ref.at[j], ref.at[j], send.at[1], recv.at[1], i, partner)
            self.onward = remote(ref.at[far], ref.at[far], send.at[2], recv.at[2], i, partner)
            self.across = [
                remote(
                    ref.at[s, :, back_half], out.at[1, s],
                    p_send.at[base + k], p_recv.at[base + k], other, j,
                )
                for k, s in enumerate((j, far))
            ]
            self.across_on = [
                remote(
                    out.at[1, s], out.at[1, s],
                    p_send.at[base + 2 + k], p_recv.at[base + 2 + k], i, partner,
                )
                for k, s in enumerate((j, far))
            ]

        def start(self):
            self.out_far.start()
            self.out_partner.start()
            self.across[0].start()

        def relay(self):
            self.out_far.wait_recv()
            self.onward.start()
            self.across[1].start()

        def relay_across(self):
            for k in range(2):
                self.across[k].wait_recv()
                self.across_on[k].start()

        def all(self):
            return [self.out_far, self.out_partner, self.onward] + self.across + self.across_on

    levels = Gathered(lvl, lvl_o, s_l, r_l, s_p, r_p, 0)
    levels.start()
    down_out[1].wait_recv()
    down_on[1].start()
    locals_[1].wait()
    locals_[2].wait()
    up_on[0].wait_recv()
    up_on[1].wait_recv()

    pair = j // 2
    pairs = (pair, (pair + 1) % 2)

    def rows_of(p):
        return pl.ds(pl.multiple_of(p * 2 * own, 128), 2 * own)

    branch_out, across = [], []
    own_rows = None
    for t in range(2):
        p = pairs[t]
        if t == 0:
            levels.out_partner.wait_recv()
        else:
            levels.onward.wait_recv()
        pre = _dot(lvl[pl.ds(p * 2, 2)].reshape(2 * own, c4), up[...])
        cdf = 0.5 * (1.0 + lax.erf(pre * np.float32(np.sqrt(0.5))))
        hidden = (pre * cdf).astype(bf16)
        hid[rows_of(p), :] = hidden
        dgel[rows_of(p), :] = cdf + pre * (jnp.exp(-0.5 * pre * pre) * np.float32(1 / np.sqrt(2 * np.pi)))
        if t == 0:
            levels.relay()
            down_on[0].wait_recv()
            down_on[1].wait_recv()
        out = jnp.concatenate([_dot(hidden, down[k]) for k in range(ni)], axis=1)
        bsend[pl.ds(p * 2, 2)] = out.astype(bf16).reshape(2, own, c4)
        cp = remote(
            bsend.at[(partner, far_partner)[t]], brecv.at[t], s_d.at[t], r_d.at[t], i, partner
        )
        cp.start()
        branch_out.append(cp)
        cp = remote(
            hid.at[rows_of(p), :], hid_o.at[1, rows_of(p), :], s_p.at[8 + t], r_p.at[8 + t], other, j
        )
        cp.start()
        across.append(cp)
    keep = [
        pltpu.make_async_copy(lvl.at[:, :, my_half], lvl_o.at[0], loc.at[3]),
        pltpu.make_async_copy(hid, hid_o.at[0], loc.at[4]),
    ]
    for cp in keep:
        cp.start()
    branch_out[1].wait_recv()
    brecv[3] = (bsend[far].astype(f32) + brecv[1].astype(f32)).astype(bf16)
    branch_out.append(remote(brecv.at[3], brecv.at[2], s_d.at[2], r_d.at[2], i, far))
    branch_out[2].start()
    branch_out[0].wait_recv()
    total = bsend[j].astype(f32) + brecv[0].astype(f32)
    branch_out[2].wait_recv()
    total = total + brecv[2].astype(f32)
    norm, inverse = _ln(total)
    coarse[...] = level + norm
    g = cot[...].astype(f32)
    slope = inverse * (
        g - jnp.mean(g, axis=-1, keepdims=True) - norm * jnp.mean(g * norm, axis=-1, keepdims=True)
    )
    slo[j] = slope.astype(bf16)
    slopes = Gathered(slo, slo_o, s_s, r_s, s_p, r_p, 4)
    slopes.start()
    levels.relay_across()
    grad_out = []
    for t in range(2):
        p = pairs[t]
        if t == 0:
            slopes.out_partner.wait_recv()
        else:
            slopes.onward.wait_recv()
        so = slo[pl.ds(p * 2, 2)].reshape(2 * own, c4)
        back = _dot(so[:, :half], down[0], 1, 1)
        for k in range(1, ni):
            back = back + _dot(so[:, k * half:(k + 1) * half], down[k], 1, 1)
        sp = (dgel[rows_of(p), :] * back).astype(bf16)
        spre[rows_of(p), :] = sp
        if t == 0:
            slopes.relay()
        cp = remote(
            spre.at[rows_of(p), :], spre_o.at[1, rows_of(p), :],
            s_p.at[10 + t], r_p.at[10 + t], other, j,
        )
        cp.start()
        across.append(cp)
        out = _dot(sp, up[...], 1, 1)
        gsend[pl.ds(p * 2, 2)] = out.astype(bf16).reshape(2, own, c4)
        for k in ((0,) if t == 0 else (1, 2)):
            cp = remote(gsend.at[peers[k]], grecv.at[j], s_g.at[k], r_g.at[k], i, peers[k])
            cp.start()
            grad_out.append(cp)
    keep += [
        pltpu.make_async_copy(slo.at[:, :, my_half], slo_o.at[0], loc.at[5]),
        pltpu.make_async_copy(spre, spre_o.at[0], loc.at[6]),
    ]
    keep[2].start()
    keep[3].start()
    slopes.relay_across()
    total = gsend[j].astype(f32)
    for k in range(3):
        grad_out[k].wait_recv()
        total = total + grecv[peers[k]].astype(f32)
    gcoarse[...] = g + total
    for cp in levels.across_on + slopes.across_on + across:
        cp.wait_recv()
    for cp in keep:
        cp.wait()
    weights = merge_far + merge_on + [merge_beside] + up_out + up_on + down_out + down_on
    sent = quads + weights + returns
    for cp in sent + levels.all() + branch_out + slopes.all() + grad_out + across:
        cp.wait_send()


def weight_kernel(coarse_in, gcoarse_in, lvl, hid, slo, spre, coarse, gcoarse, gup, gdown):
    coarse[...] = coarse_in[...]
    gcoarse[...] = gcoarse_in[...]
    gup[...] = _dot(lvl[...], spre[...], 0, 0)
    gdown[...] = _dot(hid[...], slo[...], 0, 0)


def fused(fields, logit_scale, w_qkv, w_proj, w_merge, w_up, w_down, cotangent):
    tile_rows, tile_cols, ch = fields.shape
    ni, nj = lax.axis_size("rows"), lax.axis_size("cols")
    own = cotangent.shape[0] * cotangent.shape[1]
    c4 = cotangent.shape[-1]
    half, ff = w_up.shape
    f32, bf16 = jnp.float32, jnp.bfloat16
    quad = (WIN // 2) ** 2
    vm = pl.BlockSpec(memory_space=pltpu.VMEM)
    hb = pl.BlockSpec(memory_space=pl.ANY)
    dma = pltpu.SemaphoreType.DMA
    band = nj * own
    acts = (
        jax.ShapeDtypeStruct((ni, nj, own, half), bf16),
        jax.ShapeDtypeStruct((ni, band, ff), bf16),
        jax.ShapeDtypeStruct((ni, nj, own, half), bf16),
        jax.ShapeDtypeStruct((ni, band, ff), bf16),
    )
    grid = (jax.ShapeDtypeStruct((own, c4), f32),) * 2
    outs = pl.pallas_call(
        fused_kernel,
        out_shape=grid + acts,
        in_specs=[vm, pl.BlockSpec(memory_space=pltpu.SMEM), vm, vm, hb, hb, hb, vm],
        out_specs=(vm, vm, hb, hb, hb, hb),
        scratch_shapes=[
            pltpu.VMEM((3, quad, ch), bf16),
            pltpu.VMEM((4, quad, ch), bf16),
            pltpu.VMEM((4, quad, ch), bf16),
            pltpu.VMEM((4, quad, ch), bf16),
            pltpu.VMEM((c4, w_merge.shape[0]), bf16),
            pltpu.VMEM((c4, ff), bf16),
            pltpu.VMEM((ni, ff, half), bf16),
            pltpu.VMEM((nj, own, c4), bf16),
            pltpu.VMEM((band, ff), bf16),
            pltpu.VMEM((band, ff), f32),
            pltpu.VMEM((nj, own, c4), bf16),
            pltpu.VMEM((nj, own, c4), bf16),
            pltpu.VMEM((nj, own, c4), bf16),
            pltpu.VMEM((band, ff), bf16),
            pltpu.VMEM((nj, own, c4), bf16),
            pltpu.VMEM((nj, own, c4), bf16),
            dma((7,)),
            dma((3,)), dma((3,)), dma((3,)), dma((3,)), dma((13,)), dma((13,)),
            dma((3,)), dma((3,)), dma((3,)), dma((3,)), dma((3,)), dma((3,)),
            dma((3,)), dma((3,)), dma((12,)), dma((12,)),
        ],
        compiler_params=pltpu.CompilerParams(collective_id=0, has_side_effects=True),
    )(fields, logit_scale, w_qkv, w_proj, w_merge.T, w_up, w_down, cotangent.reshape(own, c4))
    tokens = ni * band
    flat = (
        outs[0], outs[1], outs[2].reshape(tokens, half), outs[3].reshape(tokens, ff),
        outs[4].reshape(tokens, half), outs[5].reshape(tokens, ff),
    )
    outs = pl.pallas_call(
        weight_kernel,
        out_shape=grid
        + (jax.ShapeDtypeStruct((half, ff), f32), jax.ShapeDtypeStruct((ff, half), f32)),
        in_specs=[vm] * 6,
        out_specs=(vm,) * 4,
    )(*flat)
    shape = (tile_rows // 2, tile_cols // 2, c4)
    return outs[0].reshape(shape), outs[1].reshape(shape), outs[2], outs[3]


def device_body(*args):
    fields, _, w_qkv, _, w_merge, w_up, w_down, _ = args
    fits = (
        lax.axis_size("rows") == 2
        and lax.axis_size("cols") == 4
        and lax.axis_size("dp") % 2 == 0
        and fields.shape[:2] == (WIN, WIN)
        and w_up.shape[0] % 128 == 0
        and fields.shape[-1] % 128 == 0
    )
    return fused(*args) if fits else local(*args)


def solution(mesh):
    return jax.shard_map(
        device_body,
        mesh=mesh,
        in_specs=(
            P(("dp", "rows"), "cols", None),
            P(),
            P(),
            P(),
            P(None, "cols"),
            P("rows", "cols"),
            P("cols", "rows"),
            P(("dp", "rows"), "cols", None),
        ),
        out_specs=(
            P(("dp", "rows"), "cols", None),
            P(("dp", "rows"), "cols", None),
            P("rows", ("dp", "cols")),
            P("cols", ("dp", "rows")),
        ),
        check_vma=False,
    )
```
